128 devices in a mesh: row: 16 (over y, z), col: 8 (over x, core).
Axes of the slice: x: 4, y: 4, z: 4, core: 2. Of those that a mesh axis runs over, the one named last changes fastest.
Arguments:
- noise: float32 [16384, 512], P(('row', 'col')), may hold values from -40 to 40
- data: float32 [16384, 512], P(('col', 'row')), may hold values from -6 to 6
Outputs:
- noise_target: float32 [16384, 512], P(('row', 'col'))
- data_target: float32 [16384, 512], P(('col', 'row'))
- f_potential: float32 [16384], P('row')
- g_potential: float32 [16384], P('col')
The draws below stay inside these ranges and needn't reach their ends.
All inputs are finite; a program needn't handle non-finite values.
Results may differ from the reference program's by a relative error of at most 0.0003.
Values sent between devices are 32-bit elements; how exact they have to be, the bound alone decides.
No kernel may reach another device: no remote copies, remote signals or barrier semaphores. Data moves between devices by JAX's collectives and lax.ppermute only.
A program may use at most 64 MiB of HBM per device.

```python
import jax
import jax.numpy as jnp
from jax import lax

W = 512
ITERS = 2
ROWS_DEV = 1024
COLS_DEV = 2048
NOISE = 16384
DATA = 16384


def draw_noise(key, part):
    base = jnp.clip(jax.random.normal(key, (NOISE, W), jnp.float32), -5.0, 5.0)
    return base


def block_scale(rng, shape, cuts, smallest, high):
    loudness, own = 1.0, jax.random.fold_in(rng, 6)
    for dim, blocks in cuts:
        draws = jnp.exp(jax.random.uniform(jax.random.fold_in(own, dim), (blocks,), jnp.float32, smallest / len(cuts), high / len(cuts)))
        loudness = loudness * jnp.repeat(draws, shape[dim] // blocks).reshape([-1 if axis == dim else 1 for axis in range(len(shape))])
    return loudness


def gaussian(stream_key, dims, deviation, limit, cuts=(), held_as=jnp.bfloat16):
    drawn = deviation * jax.random.normal(stream_key, dims, jnp.float32)
    if cuts:
        drawn = drawn * block_scale(stream_key, dims, cuts, -0.22, 0.18)
    return jnp.clip(drawn, -limit, limit).astype(held_as)


def setup_inputs(seed: int = 0) -> dict:
    arg_keys = jax.random.split(jax.random.key(seed), 3)
    return {
        "noise": draw_noise(jax.random.fold_in(arg_keys[2], 71), 0),
        "data": gaussian(arg_keys[1], (DATA, W), 1.0, 6.0, ((0, 128),), jnp.float32),
    }


EPSILON = 32.0


def costs(xb, yb):
    xn = jnp.sum(xb * xb, axis=1)
    yn = jnp.sum(yb * yb, axis=1)
    inner = jnp.dot(xb, yb.T, precision=lax.Precision.HIGHEST, preferred_element_type=jnp.float32)
    return xn[:, None] + yn[None, :] - 2.0 * inner


def row_pass(noise, data, g_now):
    blocks = noise.reshape(NOISE // ROWS_DEV, ROWS_DEV, W)

    def single(xb):
        scores = (g_now[None, :] - costs(xb, data)) / EPSILON
        peak = jnp.max(scores, axis=1)
        expo = jnp.exp(scores - peak[:, None])
        total = jnp.sum(expo, axis=1)
        f_part = -EPSILON * (peak + jnp.log(total))
        weights = expo / total[:, None]
        target = jnp.dot(weights, data, precision=lax.Precision.HIGHEST, preferred_element_type=jnp.float32)
        return f_part, target

    f_all, targets = lax.map(single, blocks)
    return f_all.reshape(NOISE), targets.reshape(NOISE, W)


def col_pass(noise, data, f_now):
    blocks = data.reshape(DATA // COLS_DEV, COLS_DEV, W)

    def single(yb):
        scores = (f_now[:, None] - costs(noise, yb)) / EPSILON
        peak = jnp.max(scores, axis=0)
        expo = jnp.exp(scores - peak[None, :])
        total = jnp.sum(expo, axis=0)
        g_part = -EPSILON * (peak + jnp.log(total))
        weights = expo / total[None, :]
        target = jnp.dot(weights.T, noise, precision=lax.Precision.HIGHEST, preferred_element_type=jnp.float32)
        return g_part, target

    g_all, targets = lax.map(single, blocks)
    return g_all.reshape(DATA), targets.reshape(DATA, W)


def reference(noise, data):
    g_now = jnp.zeros((DATA,), jnp.float32)
    f_now = jnp.zeros((NOISE,), jnp.float32)
    data_target = jnp.zeros((DATA, W), jnp.float32)
    for step in range(ITERS):
        f_now, unused = row_pass(noise, data, g_now)
        g_now, data_target = col_pass(noise, data, f_now)
    unused_f, noise_target = row_pass(noise, data, g_now)
    return noise_target, data_target, f_now, g_now
```

```python
import jax
import jax.numpy as jnp
from jax import lax
from jax.experimental import pallas as pl
from jax.experimental.pallas import tpu as pltpu
from jax.sharding import Mesh
from jax.sharding import PartitionSpec as P

ROW = ("row_0", "row_1")
ROW_COL = ("row_0", "row_1", "col")
COL_ROW = ("col", "row_0", "row_1")

EPSILON = 32.0
LOG2E = 1.4426950408889634
LN2 = 0.6931471805599453
SCALE = LOG2E / EPSILON
BLOCK = 256
VMEM_LIMIT = 48 * 1024 * 1024


def from_everyone(shard, axis):
    size = lax.axis_size(axis)
    return lax.all_to_all(
        jnp.broadcast_to(shard[None], (size, *shard.shape)), axis, 0, 0, tiled=True
    )


def split(v):
    high = v.astype(jnp.bfloat16)
    return high, (v - high.astype(jnp.float32)).astype(jnp.bfloat16)


def dot(a, b, dims):
    return lax.dot_general(a, b, (dims, ((), ())), preferred_element_type=jnp.float32)


def as_column(row):
    return jnp.broadcast_to(row, (128, row.shape[1])).T


def as_row(column):
    return column.T[0:1, :]


def call(kernel, grid, in_specs, out_specs, out_shape, scratch=(), cost=None):
    return pl.pallas_call(
        kernel,
        grid=grid,
        in_specs=in_specs,
        out_specs=out_specs,
        out_shape=out_shape,
        scratch_shapes=scratch,
        cost_estimate=cost,
        compiler_params=pltpu.CompilerParams(
            dimension_semantics=("arbitrary",), vmem_limit_bytes=VMEM_LIMIT
        ),
    )


def whole(shape):
    return pl.BlockSpec(shape, lambda j: (0,) * len(shape))


def f32(*shape):
    return jax.ShapeDtypeStruct(shape, jnp.float32)


def scores_kernel(x_ref, y_ref, s_ref, lse_ref, xh, xl, peak, scores, bias):
    j = pl.program_id(0)
    last = pl.num_programs(0) - 1

    @pl.when(j == 0)
    def _():
        xh[...], xl[...] = split(x_ref[...] * (2.0 * SCALE))
        peak[...] = jnp.full_like(peak, -jnp.inf)

    y = y_ref[...]
    yh, yl = split(y)
    lanes = ((1,), (1,))
    s = dot(xh[...], yh, lanes) + (dot(xh[...], yl, lanes) + dot(xl[...], yh, lanes))
    norm = as_row(jnp.broadcast_to(jnp.sum(y * y, axis=1, keepdims=True), (BLOCK, 128)))
    shift = -SCALE * norm
    s_ref[...] = s
    scores[j] = s
    bias[j] = jnp.broadcast_to(shift, (8, BLOCK))
    t = s + shift
    peak[...] = jnp.maximum(peak[...], jnp.maximum(t[:, :128], t[:, 128:]))

    @pl.when(j == last)
    def _():
        top = jnp.max(peak[...], axis=1, keepdims=True)

        def add(k, total):
            e = jnp.exp2(scores[k] + (bias[k][0:1, :] - top))
            return total + (e[:, :128] + e[:, 128:])

        total = lax.fori_loop(0, pl.num_programs(0), add, jnp.zeros_like(peak))
        total = jnp.sum(total, axis=1, keepdims=True)
        lse = top + jnp.log2(total)
        lse_ref[...] = as_row(jnp.broadcast_to(lse, peak.shape))


def scores_of(x, y):
    n, w = x.shape
    m = y.shape[0]
    steps = m // BLOCK
    return call(
        scores_kernel,
        (steps,),
        [whole((n, w)), pl.BlockSpec((BLOCK, w), lambda j: (j, 0))],
        [pl.BlockSpec((n, BLOCK), lambda j: (0, j)), whole((1, n))],
        (f32(n, m), f32(1, n)),
        (
            pltpu.VMEM((n, w), jnp.bfloat16),
            pltpu.VMEM((n, w), jnp.bfloat16),
            pltpu.VMEM((n, 128), jnp.float32),
            pltpu.VMEM((steps, n, BLOCK), jnp.float32),
            pltpu.VMEM((steps, 8, BLOCK), jnp.float32),
        ),
        pl.CostEstimate(flops=6 * n * m * w, bytes_accessed=4 * n * m, transcendentals=n * m),
    )(x, y)


def negative_lse(parts):
    top = jnp.max(parts, axis=0, keepdims=True)
    return -(top + jnp.log2(jnp.sum(jnp.exp2(parts - top), axis=0, keepdims=True)))


def columns_kernel(s_ref, parts_ref, qh_ref, ql_ref, top_ref, lse_ref, a_ref, a_col):
    @pl.when(pl.program_id(0) == 0)
    def _():
        a = negative_lse(parts_ref[...])
        a_ref[...] = a
        a_col[...] = as_column(a)

    a = a_col[...]
    s = s_ref[...] + jnp.concatenate([a] * (BLOCK // 128), axis=1)
    top = jnp.max(s, axis=0, keepdims=True)
    q = jnp.exp2(s - top)
    qh_ref[...], ql_ref[...] = split(q)
    top_ref[...] = top
    lse_ref[...] = top + jnp.log2(jnp.sum(q, axis=0, keepdims=True))


def columns_of(s, parts):
    n, m = s.shape
    block = pl.BlockSpec((n, BLOCK), lambda j: (0, j))
    line = pl.BlockSpec((1, BLOCK), lambda j: (0, j))
    return call(
        columns_kernel,
        (m // BLOCK,),
        [block, whole(parts.shape)],
        [block, block, line, line, whole((1, n))],
        (
            jax.ShapeDtypeStruct((n, m), jnp.bfloat16),
            jax.ShapeDtypeStruct((n, m), jnp.bfloat16),
            f32(1, m),
            f32(1, m),
            f32(1, n),
        ),
        (pltpu.VMEM((n, 128), jnp.float32),),
        pl.CostEstimate(flops=4 * n * m, bytes_accessed=8 * n * m, transcendentals=n * m),
    )(s, parts)


def rows_kernel(qh_ref, ql_ref, top_ref, parts_ref, sum_ref, t_ref, b_ref, total):
    j = pl.program_id(0)

    @pl.when(j == 0)
    def _():
        total[...] = jnp.zeros_like(total)

    b = negative_lse(parts_ref[...])
    t = jnp.exp2(top_ref[...] + b)
    b_ref[...] = b
    t_ref[...] = t
    p = (qh_ref[...].astype(jnp.float32) + ql_ref[...].astype(jnp.float32)) * t
    total[...] += p[:, :128] + p[:, 128:]

    @pl.when(j == pl.num_programs(0) - 1)
    def _():
        rows = jnp.sum(total[...], axis=1, keepdims=True)
        sum_ref[...] = as_row(jnp.broadcast_to(rows, total.shape))


def row_sums(qh, ql, top, parts):
    n, m = qh.shape
    block = pl.BlockSpec((n, BLOCK), lambda j: (0, j))
    line = pl.BlockSpec((1, BLOCK), lambda j: (0, j))
    return call(
        rows_kernel,
        (m // BLOCK,),
        [block, block, line, pl.BlockSpec((parts.shape[0], BLOCK), lambda j: (0, j))],
        [whole((1, n)), line, line],
        (f32(1, n), f32(1, m), f32(1, m)),
        (pltpu.VMEM((n, 128), jnp.float32),),
        pl.CostEstimate(flops=4 * n * m, bytes_accessed=4 * n * m, transcendentals=0),
    )(qh, ql, top, parts)


def column_sums_kernel(qh_ref, ql_ref, parts_ref, t_ref, sum_ref, r_ref, inv):
    @pl.when(pl.program_id(0) == 0)
    def _():
        r = jnp.sum(parts_ref[...], axis=0, keepdims=True)
        r_ref[...] = r
        inv[...] = as_column(1.0 / r)

    scale = jnp.concatenate([inv[...]] * (BLOCK // 128), axis=1)
    q = (qh_ref[...].astype(jnp.float32) + ql_ref[...].astype(jnp.float32)) * scale
    sum_ref[...] = jnp.sum(q, axis=0, keepdims=True) * t_ref[...]


def column_sums(qh, ql, parts, t):
    n, m = qh.shape
    block = pl.BlockSpec((n, BLOCK), lambda j: (0, j))
    line = pl.BlockSpec((1, BLOCK), lambda j: (0, j))
    return call(
        column_sums_kernel,
        (m // BLOCK,),
        [block, block, whole(parts.shape), line],
        [line, whole((1, n))],
        (f32(1, m), f32(1, n)),
        (pltpu.VMEM((n, 128), jnp.float32),),
        pl.CostEstimate(flops=4 * n * m, bytes_accessed=4 * n * m, transcendentals=0),
    )(qh, ql, parts, t)


def data_kernel(qh_ref, ql_ref, t_ref, r_ref, x_ref, out_ref, xt):
    w = x_ref.shape[1]

    @pl.when(pl.program_id(0) == 0)
    def _():
        inv = as_column(1.0 / r_ref[...])
        scaled = x_ref[...] * jnp.concatenate([inv] * (w // 128), axis=1)
        high, low = split(scaled.T)
        xt[:w, :] = high
        xt[w:, :] = low

    inner = ((1,), (0,))
    both = dot(xt[...], qh_ref[...], inner)
    part = both[:w] + (both[w:] + dot(xt[:w, :], ql_ref[...], inner))
    out_ref[...] = (part * t_ref[...]).T


def data_part_of(qh, ql, t, r, x):
    n, m = qh.shape
    w = x.shape[1]
    block = pl.BlockSpec((n, BLOCK), lambda j: (0, j))
    return call(
        data_kernel,
        (m // BLOCK,),
        [
            block,
            block,
            pl.BlockSpec((1, BLOCK), lambda j: (0, j)),
            whole((1, n)),
            whole((n, w)),
        ],
        pl.BlockSpec((BLOCK, w), lambda j: (j, 0)),
        f32(m, w),
        (pltpu.VMEM((2 * w, n), jnp.bfloat16),),
        pl.CostEstimate(flops=6 * n * m * w, bytes_accessed=4 * n * m, transcendentals=0),
    )(qh, ql, t, r, x)


def noise_kernel(qh_ref, ql_ref, parts_ref, t_ref, y_ref, out_ref, c_ref, acc, total):
    j = pl.program_id(0)
    w = y_ref.shape[1]

    @pl.when(j == 0)
    def _():
        acc[...] = jnp.zeros_like(acc)
        total[...] = jnp.zeros_like(total)

    c = jnp.sum(parts_ref[...], axis=0, keepdims=True)
    c_ref[...] = c
    scale = t_ref[...] / c
    yh, yl = split(y_ref[...] * jnp.concatenate([as_column(scale)] * (w // 128), axis=1))
    qh, ql = qh_ref[...], ql_ref[...]
    inner = ((1,), (0,))
    acc[...] += dot(qh, yh, inner) + (dot(qh, yl, inner) + dot(ql, yh, inner))
    p = (qh.astype(jnp.float32) + ql.astype(jnp.float32)) * scale
    total[...] += p[:, :128] + p[:, 128:]

    @pl.when(j == pl.num_programs(0) - 1)
    def _():
        rows = jnp.sum(total[...], axis=1, keepdims=True)
        line = as_row(jnp.broadcast_to(rows, total.shape))
        for k in range(out_ref.shape[0]):
            at = slice(k * 128, (k + 1) * 128)
            out_ref[k, :128, :] = acc[at, :]
            out_ref[k, 128:, :] = jnp.broadcast_to(
                jnp.concatenate([line[:, at]] * (w // 128), axis=1), (8, w)
            )


def noise_part_of(qh, ql, parts, t, y):
    n, m = qh.shape
    w = y.shape[1]
    block = pl.BlockSpec((n, BLOCK), lambda j: (0, j))
    line = pl.BlockSpec((1, BLOCK), lambda j: (0, j))
    return call(
        noise_kernel,
        (m // BLOCK,),
        [
            block,
            block,
            pl.BlockSpec((parts.shape[0], BLOCK), lambda j: (0, j)),
            line,
            pl.BlockSpec((BLOCK, w), lambda j: (j, 0)),
        ],
        [whole((n // 128, 136, w)), line],
        (f32(n // 128, 136, w), f32(1, m)),
        (pltpu.VMEM((n, w), jnp.float32), pltpu.VMEM((n, 128), jnp.float32)),
        pl.CostEstimate(flops=6 * n * m * w, bytes_accessed=4 * n * m, transcendentals=0),
    )(qh, ql, parts, t, y)


def gathered(line, axis):
    n = line.shape[1]
    return from_everyone(line.reshape(n // 128, 128), axis).reshape(-1, n)


def shards(noise, data):
    x = from_everyone(noise, "col").reshape(-1, noise.shape[1])
    y = lax.all_gather(data, ROW, axis=0, tiled=True)
    s, row_lse = scores_of(x, y)
    qh, ql, top, col_lse, a = columns_of(s, gathered(row_lse, "col"))
    row_part, t, b = row_sums(qh, ql, top, gathered(col_lse, ROW))
    col_part, r = column_sums(qh, ql, gathered(row_part, "col"), t)
    data_part = data_part_of(qh, ql, t, r, x)
    for axis in ROW:
        data_part = lax.psum_scatter(data_part, axis, scatter_dimension=0, tiled=True)
    noise_part, c = noise_part_of(qh, ql, gathered(col_part, ROW), t, y)
    noise_sum = jnp.sum(lax.all_to_all(noise_part, "col", 0, 0, tiled=True), axis=0)
    noise_target = noise_sum[:128] / noise_sum[128, :128][:, None]
    x_norm = jnp.sum(x * x, axis=1)
    y_norm = jnp.sum(y * y, axis=1)
    me = lax.axis_index(ROW)
    mine = lax.dynamic_slice(c, (0, me * 128), (1, 128))
    data_target = data_part / mine.reshape(128, 1)
    f = x_norm + (LN2 * EPSILON) * (a - jnp.log2(r)).reshape(-1)
    g = y_norm + (LN2 * EPSILON) * (b - jnp.log2(c)).reshape(-1)
    return noise_target, data_target, f, g


def solution(mesh):
    torus = Mesh(mesh.devices.reshape(4, 4, mesh.shape["col"]), ("row_0", "row_1", "col"))
    placed = (P(ROW_COL, None), P(COL_ROW, None))
    return jax.shard_map(
        shards,
        mesh=torus,
        in_specs=placed,
        out_specs=(P(ROW_COL, None), P(COL_ROW, None), P(ROW), P("col")),
        check_vma=False,
    )
```

```python
import jax
import jax.numpy as jnp
from jax import lax
from jax.experimental import pallas as pl
from jax.experimental.pallas import tpu as pltpu
from jax.sharding import Mesh
from jax.sharding import PartitionSpec as P

ALL = ("y", "z", "x", "c")
PAIRS_A = ((0, 1), (2, 3))
PAIRS_B = ((1, 2), (0, 3))
UP = [(i, (i + 1) % 4) for i in range(4)]
DOWN = [(i, (i - 1) % 4) for i in range(4)]
CORES = [(0, 1), (1, 0)]


def place(y, z, x, c):
    return ((y * 4 + z) * 4 + x) * 2 + c


SAME_ROWS = [
    [place(y, z, x, c) for y in pair for x in range(4)]
    for pair in PAIRS_A
    for z in range(4)
    for c in range(2)
]
SAME_COLUMNS = [
    [place(y, z, x, c) for y in pair for z in range(4)]
    for pair in PAIRS_B
    for x in range(4)
    for c in range(2)
]

EPSILON = 32.0
LOG2E = 1.4426950408889634
LN2 = 0.6931471805599453
SCALE = LOG2E / EPSILON
BLOCK = 256
CHUNK = 64
VMEM_LIMIT = 32 * 1024 * 1024


def split(v):
    high = v.astype(jnp.bfloat16)
    return high, (v - high.astype(jnp.float32)).astype(jnp.bfloat16)


def dot(a, b, dims):
    return lax.dot_general(a, b, (dims, ((), ())), preferred_element_type=jnp.float32)


def as_column(row):
    return jnp.broadcast_to(row, (128, row.shape[1])).T


def as_row(column):
    return column.T[0:1, :]


def call(
    kernel, arrays, out_shape, scratch=(), flops=0, transcendentals=0, scalars=(), far=(), far_out=0
):
    anywhere = pl.BlockSpec(memory_space=pltpu.HBM)
    vmem = pl.BlockSpec(memory_space=pltpu.VMEM)
    smem = pl.BlockSpec(memory_space=pltpu.SMEM)
    moved = sum(v.size * v.dtype.itemsize for v in (*far, *arrays, *out_shape))
    return pl.pallas_call(
        kernel,
        in_specs=[smem] * len(scalars) + [anywhere] * len(far) + [vmem] * len(arrays),
        out_specs=[anywhere] * far_out + [vmem] * (len(out_shape) - far_out),
        out_shape=[
            pltpu.HBM(v.shape, v.dtype) if k < far_out else v for k, v in enumerate(out_shape)
        ],
        scratch_shapes=scratch,
        cost_estimate=pl.CostEstimate(
            flops=flops, bytes_accessed=moved, transcendentals=transcendentals
        ),
        compiler_params=pltpu.CompilerParams(vmem_limit_bytes=VMEM_LIMIT),
    )(*scalars, *(pltpu.with_memory_space_constraint(v, pltpu.HBM) for v in far), *arrays)


def started(copies):
    for copy in copies:
        copy.start()
    return copies


def matrix_scratch(n, m):
    half = pltpu.VMEM((m // BLOCK, n, BLOCK), jnp.bfloat16)
    return half, half, pltpu.SemaphoreType.DMA((2, m // BLOCK))


def fetched(high_from, low_from, high, low, arrived, first=0):
    return [
        started(
            [
                pltpu.make_async_copy(a.at[first + j], b.at[j], arrived.at[side, j])
                for side, (a, b) in enumerate(((high_from, high), (low_from, low)))
            ]
        )
        for j in range(high.shape[0])
    ]


def wait(copies):
    for copy in copies:
        copy.wait()


def span(k, size):
    return pl.ds(pl.multiple_of(k * size, size), size)


def f32(*shape):
    return jax.ShapeDtypeStruct(shape, jnp.float32)


def scores_kernel(*refs):
    slots, xs, ys = refs[0], refs[1:9], refs[9:25]
    xt_out, s_ref, lse_ref, xn_ref, yn_ref = refs[25:30]
    xk, yk, peak, total, x, y, xt, arrived, sent = refs[30:]
    n, m = s_ref.shape
    w = y.shape[1]
    steps = m // BLOCK

    def norms(v):
        return as_row(jnp.broadcast_to(jnp.sum(v * v, axis=1, keepdims=True), (128, 128)))

    here = [x.at[pl.ds(k * 128, 128)] for k in range(8)] + [
        y.at[pl.ds(k * 128, 128)] for k in range(16)
    ]
    copies = started(
        [
            pltpu.make_async_copy(a, b, arrived.at[k])
            for k, (a, b) in enumerate(zip((*xs, *ys), here))
        ]
    )
    for k in range(8):
        at = span(slots[k], 128)
        copies[k].wait()
        v = here[k][...]
        xt[:, at] = v.T
        xn_ref[:, at] = norms(v)
        high, low = split(v * (2.0 * SCALE))
        xk[at, :w] = high
        xk[at, w : 2 * w] = high
        xk[at, 2 * w :] = low
    kept = pltpu.make_async_copy(xt, xt_out, sent)
    kept.start()
    for k in range(16):
        at = span(slots[8 + k], 128)
        copies[8 + k].wait()
        v = here[8 + k][...]
        yn_ref[:, at] = norms(v)
        high, low = split(v)
        yk[at, :w] = high
        yk[at, w : 2 * w] = low
        yk[at, 2 * w :] = high
    peak[...] = jnp.full_like(peak, -jnp.inf)
    total[...] = jnp.zeros_like(total)

    def multiply(j):
        at = span(j, BLOCK)
        s_ref[:, at] = dot(xk[...], yk[at, :], ((1,), (1,)))

    def collect(j):
        at = span(j, BLOCK)
        shift = SCALE * yn_ref[:, at]
        for i in range(0, n, CHUNK):
            rows = slice(i, i + CHUNK)
            t = s_ref[rows, at] - shift
            old = peak[rows, :]
            new = jnp.maximum(old, jnp.maximum(t[:, :128], t[:, 128:]))
            part = jnp.exp2(t[:, :128] - new) + jnp.exp2(t[:, 128:] - new)
            total[rows, :] = total[rows, :] * jnp.exp2(old - new) + part
            peak[rows, :] = new

    multiply(0)

    def step(j, carry):
        multiply(j)
        collect(j - 1)
        return carry

    lax.fori_loop(1, steps, step, 0)
    collect(steps - 1)
    top = jnp.max(peak[...], axis=1, keepdims=True)
    sums = jnp.sum(total[...] * jnp.exp2(peak[...] - top), axis=1, keepdims=True)
    lse_ref[...] = as_row(jnp.broadcast_to(top + jnp.log2(sums), peak.shape))
    kept.wait()


def scores_of(slots, xs, ys):
    n, m, w = 8 * 128, 16 * 128, xs[0].shape[1]
    return call(
        scores_kernel,
        (),
        (f32(w, n), f32(n, m), f32(1, n), f32(1, n), f32(1, m)),
        (
            pltpu.VMEM((n, 3 * w), jnp.bfloat16),
            pltpu.VMEM((m, 3 * w), jnp.bfloat16),
            pltpu.VMEM((n, 128), jnp.float32),
            pltpu.VMEM((n, 128), jnp.float32),
            pltpu.VMEM((n, w), jnp.float32),
            pltpu.VMEM((m, w), jnp.float32),
            pltpu.VMEM((w, n), jnp.float32),
            pltpu.SemaphoreType.DMA((24,)),
            pltpu.SemaphoreType.DMA,
        ),
        flops=6 * n * m * w,
        transcendentals=n * m,
        scalars=(slots,),
        far=(*xs, *ys),
        far_out=1,
    )


def negative_lse(parts):
    top = jnp.max(parts, axis=0, keepdims=True)
    return -(top + jnp.log2(jnp.sum(jnp.exp2(parts - top), axis=0, keepdims=True)))


def columns_kernel(
    s_ref, parts_ref, high_out, low_out, top_ref, lse_ref, a_ref, a_col, qh_ref, ql_ref, sent
):
    n, m = s_ref.shape
    a = negative_lse(parts_ref[...])
    a_ref[...] = a
    a_col[...] = as_column(a)

    def shifted(i, at):
        a = a_col[i : i + CHUNK, :]
        return s_ref[i : i + CHUNK, at] + jnp.concatenate([a] * (BLOCK // 128), axis=1)

    def folded(v, op):
        return op(v.reshape(CHUNK // 8, 8, BLOCK), axis=0)

    def step(j, carry):
        at = span(j, BLOCK)
        top = jnp.full((8, BLOCK), -jnp.inf, jnp.float32)
        for i in range(0, n, CHUNK):
            top = jnp.maximum(top, folded(shifted(i, at), jnp.max))
        top = jnp.max(top, axis=0, keepdims=True)
        total = jnp.zeros((8, BLOCK), jnp.float32)
        for i in range(0, n, CHUNK):
            q = jnp.exp2(shifted(i, at) - top)
            total = total + folded(q, jnp.sum)
            qh_ref[j, i : i + CHUNK, :], ql_ref[j, i : i + CHUNK, :] = split(q)
        top_ref[:, at] = top
        lse_ref[:, at] = top + jnp.log2(jnp.sum(total, axis=0, keepdims=True))
        started(kept(j))
        return carry

    def kept(j):
        return [
            pltpu.make_async_copy(a.at[j], b.at[j], sent.at[side, j])
            for side, (a, b) in enumerate(((qh_ref, high_out), (ql_ref, low_out)))
        ]

    lax.fori_loop(0, m // BLOCK, step, 0)
    for j in range(m // BLOCK):
        wait(kept(j))


def columns_of(s, parts):
    n, m = s.shape
    half = jax.ShapeDtypeStruct((m // BLOCK, n, BLOCK), jnp.bfloat16)
    return call(
        columns_kernel,
        (s, parts),
        (half, half, f32(1, m), f32(1, m), f32(1, n)),
        (
            pltpu.VMEM((n, 128), jnp.float32),
            *matrix_scratch(n, m),
        ),
        flops=4 * n * m,
        transcendentals=n * m,
        far_out=2,
    )


def joint(high, low):
    return high.astype(jnp.float32) + low.astype(jnp.float32)


def add_weighted(total, high, low, weights):
    for i in range(0, total.shape[0], CHUNK):
        rows = slice(i, i + CHUNK)
        p = joint(high[rows, :], low[rows, :]) * weights
        total[rows, :] += p[:, :128] + p[:, 128:]


def lane_sums(total):
    return as_row(jnp.broadcast_to(jnp.sum(total[...], axis=1, keepdims=True), total.shape))


def rows_kernel(
    high, low, top_ref, parts_ref, sum_ref, t_ref, b_ref, total, qh_ref, ql_ref, arrived
):
    copies = fetched(high, low, qh_ref, ql_ref, arrived)
    b = negative_lse(parts_ref[...])
    b_ref[...] = b
    t_ref[...] = jnp.exp2(top_ref[...] + b)
    total[...] = jnp.zeros_like(total)
    for j, copy in enumerate(copies):
        wait(copy)
        weights = t_ref[:, j * BLOCK : (j + 1) * BLOCK]
        add_weighted(total, qh_ref.at[j], ql_ref.at[j], weights)
    sum_ref[...] = lane_sums(total)


def row_sums(qh, ql, top, parts):
    n, m = qh.shape[1], qh.shape[0] * BLOCK
    return call(
        rows_kernel,
        (top, parts),
        (f32(1, n), f32(1, m), f32(1, m)),
        (pltpu.VMEM((n, 128), jnp.float32), *matrix_scratch(n, m)),
        flops=4 * n * m,
        far=(qh, ql),
    )


def column_sums_kernel(high, low, parts_ref, t_ref, sum_ref, r_ref, inv, qh_ref, ql_ref, arrived):
    copies = fetched(high, low, qh_ref, ql_ref, arrived)
    n = inv.shape[0]
    r = jnp.sum(parts_ref[...], axis=0, keepdims=True)
    r_ref[...] = r
    inv[...] = as_column(1.0 / r)
    for j, copy in enumerate(copies):
        wait(copy)
        total = jnp.zeros((8, BLOCK), jnp.float32)
        for i in range(0, n, CHUNK):
            rows = slice(i, i + CHUNK)
            scale = jnp.concatenate([inv[rows, :]] * (BLOCK // 128), axis=1)
            q = joint(qh_ref[j, rows, :], ql_ref[j, rows, :]) * scale
            total = total + jnp.sum(q.reshape(CHUNK // 8, 8, BLOCK), axis=0)
        at = slice(j * BLOCK, (j + 1) * BLOCK)
        sum_ref[:, at] = jnp.sum(total, axis=0, keepdims=True) * t_ref[:, at]


def column_sums(qh, ql, parts, t):
    n, m = qh.shape[1], qh.shape[0] * BLOCK
    return call(
        column_sums_kernel,
        (parts, t),
        (f32(1, m), f32(1, n)),
        (pltpu.VMEM((n, 128), jnp.float32), *matrix_scratch(n, m)),
        flops=4 * n * m,
        far=(qh, ql),
    )


def data_kernel(seats, high_from, low_from, xt_from, t_ref, r_ref, *refs):
    outs, (xt, xt_ref, come, qh_ref, ql_ref, arrived, done) = refs[:8], refs[8:]
    w = xt_ref.shape[0]
    steps = qh_ref.shape[0]
    first = pltpu.make_async_copy(xt_from, xt_ref, come)
    first.start()
    copies = fetched(high_from, low_from, qh_ref, ql_ref, arrived, seats[0] * steps)
    first.wait()
    high, low = split(xt_ref[...] * (1.0 / r_ref[...]))
    xt[:w, :] = high
    xt[w:, :] = low
    inner = ((1,), (0,))
    for j, copy in enumerate(copies):
        wait(copy)
        scale = t_ref[:, span(seats[0] * steps + j, BLOCK)]
        both = dot(xt[...], qh_ref[j], inner)
        part = both[:w] + (both[w:] + dot(xt[:w, :], ql_ref[j], inner))
        part = (part * scale).T
        for k in range(BLOCK // 128):
            done[seats[1 + j * (BLOCK // 128) + k]] = part[k * 128 : (k + 1) * 128]
    for k in range(8):
        outs[k][...] = done[k]


def data_part_of(core, seats, qh, ql, t, r, xt):
    n, m = qh.shape[1], qh.shape[0] * BLOCK
    w = xt.shape[0]
    return call(
        data_kernel,
        (t, r),
        [f32(128, w)] * 8,
        (
            pltpu.VMEM((2 * w, n), jnp.bfloat16),
            pltpu.VMEM((w, n), jnp.float32),
            pltpu.SemaphoreType.DMA,
            *matrix_scratch(n, m // 2),
            pltpu.VMEM((8, 128, w), jnp.float32),
        ),
        flops=3 * n * m * w,
        far=(qh, ql, xt),
        scalars=(jnp.concatenate([core.reshape(1).astype(jnp.int32), seats]),),
    )


def noise_kernel(seats, high_from, low_from, *refs):
    ys, (parts_ref, t_ref), outs = refs[:16], refs[16:18], refs[18:26]
    c_ref, total, acc, y_ref, come, qh_ref, ql_ref, arrived = refs[26:]
    w = y_ref.shape[1]
    moves = started(
        [
            pltpu.make_async_copy(v, y_ref.at[span(seats[8 + k], 128)], come.at[k])
            for k, v in enumerate(ys)
        ]
    )
    copies = fetched(high_from, low_from, qh_ref, ql_ref, arrived)
    c = jnp.sum(parts_ref[...], axis=0, keepdims=True)
    c_ref[...] = c
    scale = t_ref[...] / c
    total[...] = jnp.zeros_like(total)
    inner = ((1,), (0,))
    wait(moves)
    for j, copy in enumerate(copies):
        at = slice(j * BLOCK, (j + 1) * BLOCK)
        column = jnp.concatenate([as_column(scale[:, at])] * (w // 128), axis=1)
        yh, yl = split(y_ref[at, :] * column)
        wait(copy)
        qh, ql = qh_ref[j], ql_ref[j]
        part = dot(qh, yh, inner) + (dot(qh, yl, inner) + dot(ql, yh, inner))
        if j == 0:
            acc[...] = part
        else:
            acc[...] += part
        add_weighted(total, qh_ref.at[j], ql_ref.at[j], scale[:, at])
    line = lane_sums(total)
    for seat in range(8):
        for k in range(8):

            @pl.when(seats[k] == seat)
            def _(k=k, seat=seat):
                at = slice(k * 128, (k + 1) * 128)
                outs[seat][:128, :] = acc[at, :]
                sums = jnp.concatenate([line[:, at]] * (w // 128), axis=1)
                outs[seat][128:, :] = jnp.broadcast_to(sums, (8, w))


def noise_part_of(seats, qh, ql, parts, t, ys):
    n, m = qh.shape[1], qh.shape[0] * BLOCK
    w = ys[0].shape[1]
    out = call(
        noise_kernel,
        (parts, t),
        [f32(136, w)] * 8 + [f32(1, m)],
        (
            pltpu.VMEM((n, 128), jnp.float32),
            pltpu.VMEM((n, w), jnp.float32),
            pltpu.VMEM((m, w), jnp.float32),
            pltpu.SemaphoreType.DMA((16,)),
            *matrix_scratch(n, m),
        ),
        flops=6 * n * m * w,
        far=(qh, ql, *ys),
        scalars=(seats,),
    )
    return out[:8], out[8]


def pairs(groups):
    return [p for a, b in groups for p in ((a, b), (b, a))]


def gathered(line, groups):
    n, size = line.shape[1], len(groups[0])
    mine = jnp.broadcast_to(line.reshape(1, n // 128, 128), (size, n // 128, 128))
    parts = lax.all_to_all(mine, ALL, 0, 0, axis_index_groups=groups, tiled=True)
    return parts.reshape(size, n)


def spread(own, ring, pair):
    across = pairs(pair)
    below = lax.ppermute(own, ring, UP)
    above = lax.ppermute(own, ring, DOWN)
    over = lax.ppermute(own, "y", across)
    far = lax.ppermute(below, ring, UP)
    over_below = lax.ppermute(over, ring, UP)
    over_above = lax.ppermute(over, ring, DOWN)
    over_far = lax.ppermute(far, "y", across)
    return [own, below, above, over, far, over_below, over_above, over_far]


def sum_to_owner(parts, ring, pair):
    own, up, far, down, over, over_up, over_far, over_down = parts
    across = pairs(pair)
    far = far + lax.ppermute(over_far, "y", across)
    over = over + lax.ppermute(over_up, ring, UP) + lax.ppermute(over_down, ring, DOWN)
    up = up + lax.ppermute(far, ring, UP)
    down = lax.ppermute(down, ring, DOWN)
    return own + down + lax.ppermute(over, "y", across) + lax.ppermute(up, ring, UP)


def shards(noise, data):
    iy, iz, ix, ic = (lax.axis_index(name) for name in ALL)
    row_y, col_y = iy % 2, iy // 2

    xs = spread(noise, "x", PAIRS_A)
    ys = spread(data, "z", PAIRS_B)
    ys = ys + [lax.ppermute(v, "c", CORES) for v in ys]

    hops = ((0, 0), (0, 3), (0, 1), (1, 0), (0, 2), (1, 3), (1, 1), (1, 2))
    row_slots = [(row_y ^ dy) * 4 + (ix + d) % 4 for dy, d in hops]
    col_slots = [(col_y ^ dy) * 4 + (iz + d) % 4 for dy, d in hops]
    slots = jnp.stack(
        row_slots + [ic * 8 + k for k in col_slots] + [(1 - ic) * 8 + k for k in col_slots]
    ).astype(jnp.int32)
    kk = jnp.arange(16, dtype=jnp.int32)
    row_seats = ((kk // 4) ^ row_y) * 4 + (kk - ix) % 4
    col_seats = ((kk // 4 % 2) ^ col_y) * 4 + (kk - iz) % 4

    xt, s, row_lse, xn, yn = scores_of(slots, xs, ys)
    qh, ql, top, col_lse, a = columns_of(s, gathered(row_lse, SAME_ROWS))
    other = lax.ppermute(col_lse, "c", CORES)
    peak = jnp.maximum(col_lse, other)
    col_lse = peak + jnp.log2(1.0 + jnp.exp2(jnp.minimum(col_lse, other) - peak))
    row_part, t, b = row_sums(qh, ql, top, gathered(col_lse, SAME_COLUMNS))
    col_part, r = column_sums(qh, ql, gathered(row_part, SAME_ROWS), t)
    col_part = col_part + lax.ppermute(col_part, "c", CORES)
    to_other = data_part_of(1 - ic, col_seats, qh, ql, t, r, xt)
    to_own = data_part_of(ic, col_seats, qh, ql, t, r, xt)
    shares = [v + lax.ppermute(u, "c", CORES) for u, v in zip(to_other, to_own)]
    col_part, shares = lax.optimization_barrier((col_part, shares))
    col_parts = gathered(col_part, SAME_COLUMNS)
    data_sum = sum_to_owner(shares, "z", PAIRS_B)
    noise_part, c = noise_part_of(
        jnp.concatenate([row_seats[:8], slots[8:]]), qh, ql, col_parts, t, ys
    )
    noise_sum = sum_to_owner(noise_part, "x", PAIRS_A)
    noise_target = noise_sum[:128] / noise_sum[128, :128][:, None]
    mine = lax.dynamic_slice(c, (0, (ic * 8 + col_y * 4 + iz) * 128), (1, 128))
    data_target = data_sum / mine.reshape(128, 1)

    f = (xn + (LN2 * EPSILON) * (a - jnp.log2(r))).reshape(2, 4, 128)
    f_mine = lax.dynamic_index_in_dim(f, row_y, 0, keepdims=False)
    f_other = lax.ppermute(f_mine, "c", CORES)
    f_both = jnp.where(ic == 0, jnp.stack([f_mine, f_other], 1), jnp.stack([f_other, f_mine], 1))
    g = (yn + (LN2 * EPSILON) * (b - jnp.log2(c))).reshape(2, 2, 4, 128)
    g_mine = lax.dynamic_index_in_dim(g, ic, 0, keepdims=False)
    g_other = lax.ppermute(g_mine, "y", pairs(PAIRS_A))
    outer = (iy == 0) | (iy == 3)
    g_03, g_12 = jnp.where(outer, g_mine, g_other), jnp.where(outer, g_other, g_mine)
    g_all = jnp.stack([g_03[0], g_12[0], g_12[1], g_03[1]])
    return noise_target, data_target, f_both.reshape(-1), g_all.reshape(-1)


def solution(mesh):
    torus = Mesh(mesh.devices.reshape(4, 4, 4, 2), ALL)
    return jax.shard_map(
        shards,
        mesh=torus,
        in_specs=(P(("y", "z", "x", "c"), None), P(("x", "c", "y", "z"), None)),
        out_specs=(
            P(("y", "z", "x", "c"), None),
            P(("x", "c", "y", "z"), None),
            P(("y", "z")),
            P(("x", "c")),
        ),
        check_vma=False,
    )
```

```python
import functools

import jax
import jax.numpy as jnp
from jax import lax
from jax.experimental import pallas as pl
from jax.experimental.pallas import tpu as pltpu
from jax.sharding import Mesh
from jax.sharding import PartitionSpec as P

ALL = ("y", "z", "x", "c")
PAIRS_A = ((0, 1), (2, 3))
PAIRS_B = ((1, 2), (0, 3))
UP = [(i, (i + 1) % 4) for i in range(4)]
DOWN = [(i, (i - 1) % 4) for i in range(4)]
CORES = [(0, 1), (1, 0)]


def place(y, z, x, c):
    return ((y * 4 + z) * 4 + x) * 2 + c


SAME_ROWS = [
    [place(y, z, x, c) for y in pair for x in range(4)]
    for pair in PAIRS_A
    for z in range(4)
    for c in range(2)
]
SAME_COLUMNS = [
    [place(y, z, x, c) for y in pair for z in range(4)]
    for pair in PAIRS_B
    for x in range(4)
    for c in range(2)
]

EPSILON = 32.0
LOG2E = 1.4426950408889634
LN2 = 0.6931471805599453
SCALE = LOG2E / EPSILON
BLOCK = 256
WIDE = 512
CHUNK = 64
VMEM_LIMIT = 32 * 1024 * 1024


def split(v):
    high = v.astype(jnp.bfloat16)
    return high, (v - high.astype(jnp.float32)).astype(jnp.bfloat16)


def dot(a, b, dims):
    return lax.dot_general(a, b, (dims, ((), ())), preferred_element_type=jnp.float32)


def as_column(row):
    return jnp.broadcast_to(row, (128, row.shape[1])).T


def as_row(column):
    return column.T[0:1, :]


def call(
    kernel, arrays, out_shape, scratch=(), flops=0, transcendentals=0, scalars=(), far=(), far_out=0
):
    anywhere = pl.BlockSpec(memory_space=pltpu.HBM)
    vmem = pl.BlockSpec(memory_space=pltpu.VMEM)
    smem = pl.BlockSpec(memory_space=pltpu.SMEM)
    moved = sum(v.size * v.dtype.itemsize for v in (*far, *arrays, *out_shape))
    return pl.pallas_call(
        kernel,
        in_specs=[smem] * len(scalars) + [anywhere] * len(far) + [vmem] * len(arrays),
        out_specs=[anywhere] * far_out + [vmem] * (len(out_shape) - far_out),
        out_shape=[
            pltpu.HBM(v.shape, v.dtype) if k < far_out else v for k, v in enumerate(out_shape)
        ],
        scratch_shapes=scratch,
        cost_estimate=pl.CostEstimate(
            flops=flops, bytes_accessed=moved, transcendentals=transcendentals
        ),
        compiler_params=pltpu.CompilerParams(vmem_limit_bytes=VMEM_LIMIT),
    )(*scalars, *(pltpu.with_memory_space_constraint(v, pltpu.HBM) for v in far), *arrays)


def started(copies):
    for copy in copies:
        copy.start()
    return copies


def matrix_scratch(n, m):
    half = pltpu.VMEM((m // BLOCK, n, BLOCK), jnp.bfloat16)
    return half, half, pltpu.SemaphoreType.DMA((2, m // BLOCK))


def block_copies(j, high_from, low_from, high, low, arrived, first=0):
    return [
        pltpu.make_async_copy(a.at[first + j], b.at[j], arrived.at[side, j])
        for side, (a, b) in enumerate(((high_from, high), (low_from, low)))
    ]


def wait(copies):
    for copy in copies:
        copy.wait()


def span(k, size):
    return pl.ds(pl.multiple_of(k * size, size), size)


def f32(*shape):
    return jax.ShapeDtypeStruct(shape, jnp.float32)


def scores_kernel(*refs):
    slots, xs, ys = refs[0], refs[1:9], refs[9:25]
    xt_out, s_ref, lse_ref, xn_ref, yn_ref = refs[25:30]
    xk, yk, peak, total, x, y, xt, arrived, sent = refs[30:]
    n, m = s_ref.shape
    w = y.shape[1]
    steps = m // WIDE

    def norms(v):
        return as_row(jnp.broadcast_to(jnp.sum(v * v, axis=1, keepdims=True), (128, 128)))

    here = [(x if k < 8 else y).at[span(slots[k], 128)] for k in range(24)]
    copies = started(
        [
            pltpu.make_async_copy(a, b, arrived.at[k])
            for k, (a, b) in enumerate(zip((*xs, *ys), here))
        ]
    )
    wait(copies[:8])

    def place_row_block(k, carry):
        at = span(k, 128)
        v = x[at, :]
        xt[:, at] = v.T
        xn_ref[:, at] = norms(v)
        high, low = split(v * (2.0 * SCALE))
        xk[at, :w] = high
        xk[at, w : 2 * w] = high
        xk[at, 2 * w :] = low
        return carry

    lax.fori_loop(0, 8, place_row_block, 0)
    kept = pltpu.make_async_copy(xt, xt_out, sent)
    kept.start()
    wait(copies[8:])

    def prepare(j):
        for k in range(WIDE // 128):
            at = span(j * (WIDE // 128) + k, 128)
            v = y[at, :]
            yn_ref[:, at] = norms(v)
            high, low = split(v)
            yk[at, :w] = high
            yk[at, w : 2 * w] = low
            yk[at, 2 * w :] = high

    prepare(0)
    peak[...] = jnp.full_like(peak, -jnp.inf)
    total[...] = jnp.zeros_like(total)

    def multiply(j):
        at = span(j, WIDE)
        s_ref[:, at] = dot(xk[...], yk[at, :], ((1,), (1,)))

    def collect(j):
        at = span(j, WIDE)
        shift = SCALE * yn_ref[:, at]
        for i in range(0, n, CHUNK // 2):
            rows = slice(i, i + CHUNK // 2)
            t = s_ref[rows, at] - shift
            old = peak[rows, :]
            lanes = [t[:, k : k + 128] for k in range(0, WIDE, 128)]
            new = functools.reduce(jnp.maximum, lanes, old)
            part = sum(jnp.exp2(v - new) for v in lanes)
            total[rows, :] = total[rows, :] * jnp.exp2(old - new) + part
            peak[rows, :] = new

    multiply(0)
    prepare(1)

    def step(j, carry):
        multiply(j)
        collect(j - 1)
        prepare(jnp.minimum(j + 1, steps - 1))
        return carry

    lax.fori_loop(1, steps, step, 0)
    collect(steps - 1)
    top = jnp.max(peak[...], axis=1, keepdims=True)
    sums = jnp.sum(total[...] * jnp.exp2(peak[...] - top), axis=1, keepdims=True)
    lse_ref[...] = as_row(jnp.broadcast_to(top + jnp.log2(sums), peak.shape))
    kept.wait()


def scores_of(slots, xs, ys):
    n, m, w = 8 * 128, 16 * 128, xs[0].shape[1]
    return call(
        scores_kernel,
        (),
        (f32(w, n), f32(n, m), f32(1, n), f32(1, n), f32(1, m)),
        (
            pltpu.VMEM((n, 3 * w), jnp.bfloat16),
            pltpu.VMEM((m, 3 * w), jnp.bfloat16),
            pltpu.VMEM((n, 128), jnp.float32),
            pltpu.VMEM((n, 128), jnp.float32),
            pltpu.VMEM((n, w), jnp.float32),
            pltpu.VMEM((m, w), jnp.float32),
            pltpu.VMEM((w, n), jnp.float32),
            pltpu.SemaphoreType.DMA((24,)),
            pltpu.SemaphoreType.DMA,
        ),
        flops=6 * n * m * w,
        transcendentals=n * m,
        scalars=(slots,),
        far=(*xs, *ys),
        far_out=1,
    )


def negative_lse(parts):
    top = jnp.max(parts, axis=0, keepdims=True)
    return -(top + jnp.log2(jnp.sum(jnp.exp2(parts - top), axis=0, keepdims=True)))


def columns_kernel(
    s_ref, parts_ref, high_out, low_out, top_ref, lse_ref, a_ref, a_col, qh_ref, ql_ref, sent
):
    n, m = s_ref.shape
    a = negative_lse(parts_ref[...])
    a_ref[...] = a
    a_col[...] = as_column(a)

    def shifted(i, at):
        a = a_col[i : i + CHUNK, :]
        return s_ref[i : i + CHUNK, at] + jnp.concatenate([a] * (BLOCK // 128), axis=1)

    def folded(v, op):
        return op(v.reshape(CHUNK // 8, 8, BLOCK), axis=0)

    def step(j, carry):
        at = span(j, BLOCK)
        top = jnp.full((8, BLOCK), -jnp.inf, jnp.float32)
        for i in range(0, n, CHUNK):
            top = jnp.maximum(top, folded(shifted(i, at), jnp.max))
        top = jnp.max(top, axis=0, keepdims=True)
        total = jnp.zeros((8, BLOCK), jnp.float32)
        for i in range(0, n, CHUNK):
            q = jnp.exp2(shifted(i, at) - top)
            total = total + folded(q, jnp.sum)
            qh_ref[j, i : i + CHUNK, :], ql_ref[j, i : i + CHUNK, :] = split(q)
        top_ref[:, at] = top
        lse_ref[:, at] = top + jnp.log2(jnp.sum(total, axis=0, keepdims=True))
        started(kept(j))
        return carry

    def kept(j):
        return [
            pltpu.make_async_copy(a.at[j], b.at[j], sent.at[side, j])
            for side, (a, b) in enumerate(((qh_ref, high_out), (ql_ref, low_out)))
        ]

    lax.fori_loop(0, m // BLOCK, step, 0)
    for j in range(m // BLOCK):
        wait(kept(j))


def columns_of(s, parts):
    n, m = s.shape
    half = jax.ShapeDtypeStruct((m // BLOCK, n, BLOCK), jnp.bfloat16)
    return call(
        columns_kernel,
        (s, parts),
        (half, half, f32(1, m), f32(1, m), f32(1, n)),
        (
            pltpu.VMEM((n, 128), jnp.float32),
            *matrix_scratch(n, m),
        ),
        flops=4 * n * m,
        transcendentals=n * m,
        far_out=2,
    )


def joint(high, low):
    return high.astype(jnp.float32) + low.astype(jnp.float32)


def add_weighted(total, high, low, weights):
    for i in range(0, total.shape[0], CHUNK):
        rows = slice(i, i + CHUNK)
        p = joint(high[rows, :], low[rows, :]) * weights
        total[rows, :] += p[:, :128] + p[:, 128:]


def lane_sums(total):
    return as_row(jnp.broadcast_to(jnp.sum(total[...], axis=1, keepdims=True), total.shape))


def rows_kernel(
    high, low, top_ref, parts_ref, sum_ref, t_ref, b_ref, total, qh_ref, ql_ref, arrived
):
    halves = (high, low, qh_ref, ql_ref, arrived)
    steps = qh_ref.shape[0]
    for j in range(steps):
        started(block_copies(j, *halves))
    b = negative_lse(parts_ref[...])
    b_ref[...] = b
    t_ref[...] = jnp.exp2(top_ref[...] + b)
    total[...] = jnp.zeros_like(total)

    def step(j, carry):
        wait(block_copies(j, *halves))
        add_weighted(total, qh_ref.at[j], ql_ref.at[j], t_ref[:, span(j, BLOCK)])
        return carry

    lax.fori_loop(0, steps, step, 0)
    sum_ref[...] = lane_sums(total)


def row_sums(qh, ql, top, parts):
    n, m = qh.shape[1], qh.shape[0] * BLOCK
    return call(
        rows_kernel,
        (top, parts),
        (f32(1, n), f32(1, m), f32(1, m)),
        (pltpu.VMEM((n, 128), jnp.float32), *matrix_scratch(n, m)),
        flops=4 * n * m,
        far=(qh, ql),
    )


def column_sums_kernel(high, low, parts_ref, t_ref, sum_ref, r_ref, inv, qh_ref, ql_ref, arrived):
    halves = (high, low, qh_ref, ql_ref, arrived)
    steps = qh_ref.shape[0]
    for j in range(steps):
        started(block_copies(j, *halves))
    n = inv.shape[0]
    r = jnp.sum(parts_ref[...], axis=0, keepdims=True)
    r_ref[...] = r
    inv[...] = as_column(1.0 / r)

    def step(j, carry):
        wait(block_copies(j, *halves))
        total = jnp.zeros((8, BLOCK), jnp.float32)
        for i in range(0, n, CHUNK):
            rows = slice(i, i + CHUNK)
            scale = jnp.concatenate([inv[rows, :]] * (BLOCK // 128), axis=1)
            q = joint(qh_ref[j, rows, :], ql_ref[j, rows, :]) * scale
            total = total + jnp.sum(q.reshape(CHUNK // 8, 8, BLOCK), axis=0)
        at = span(j, BLOCK)
        sum_ref[:, at] = jnp.sum(total, axis=0, keepdims=True) * t_ref[:, at]
        return carry

    lax.fori_loop(0, steps, step, 0)


def column_sums(qh, ql, parts, t):
    n, m = qh.shape[1], qh.shape[0] * BLOCK
    return call(
        column_sums_kernel,
        (parts, t),
        (f32(1, m), f32(1, n)),
        (pltpu.VMEM((n, 128), jnp.float32), *matrix_scratch(n, m)),
        flops=4 * n * m,
        far=(qh, ql),
    )


def data_kernel(seats, high_from, low_from, xt_from, t_ref, r_ref, *refs):
    outs, (xt, xt_ref, come, qh_ref, ql_ref, arrived, done) = refs[:8], refs[8:]
    w = xt_ref.shape[0]
    steps = qh_ref.shape[0]
    first = pltpu.make_async_copy(xt_from, xt_ref, come)
    first.start()
    halves = (high_from, low_from, qh_ref, ql_ref, arrived, seats[0] * steps)
    for j in range(steps):
        started(block_copies(j, *halves))
    first.wait()
    high, low = split(xt_ref[...] * (1.0 / r_ref[...]))
    n = xt_ref.shape[1]
    xt[:, :n] = high
    xt[:, n : 2 * n] = low
    xt[:, 2 * n :] = high
    inner = ((1,), (0,))

    def step(j, carry):
        wait(block_copies(2 * j, *halves))
        wait(block_copies(2 * j + 1, *halves))
        scale = t_ref[:, span(seats[0] * (steps // 2) + j, 2 * BLOCK)]
        high = jnp.concatenate([qh_ref[2 * j], qh_ref[2 * j + 1]], axis=1)
        low = jnp.concatenate([ql_ref[2 * j], ql_ref[2 * j + 1]], axis=1)
        part = dot(xt[...], jnp.concatenate([high, high, low], axis=0), inner)
        part = (part * scale).T
        for k in range(2 * BLOCK // 128):
            done[seats[1 + j * (2 * BLOCK // 128) + k]] = part[k * 128 : (k + 1) * 128]
        return carry

    lax.fori_loop(0, steps // 2, step, 0)
    for k in range(8):
        outs[k][...] = done[k]


def data_part_of(core, seats, qh, ql, t, r, xt):
    n, m = qh.shape[1], qh.shape[0] * BLOCK
    w = xt.shape[0]
    return call(
        data_kernel,
        (t, r),
        [f32(128, w)] * 8,
        (
            pltpu.VMEM((w, 3 * n), jnp.bfloat16),
            pltpu.VMEM((w, n), jnp.float32),
            pltpu.SemaphoreType.DMA,
            *matrix_scratch(n, m // 2),
            pltpu.VMEM((8, 128, w), jnp.float32),
        ),
        flops=3 * n * m * w,
        far=(qh, ql, xt),
        scalars=(jnp.concatenate([core.reshape(1).astype(jnp.int32), seats]),),
    )


def noise_kernel(seats, high_from, low_from, *refs):
    ys, (parts_ref, t_ref), outs = refs[:16], refs[16:18], refs[18:26]
    c_ref, total, acc, yk, scale, line, y_ref, come, qh_ref, ql_ref, arrived = refs[26:]
    w = y_ref.shape[1]
    moves = started(
        [
            pltpu.make_async_copy(v, y_ref.at[span(seats[8 + k], 128)], come.at[k])
            for k, v in enumerate(ys)
        ]
    )
    halves = (high_from, low_from, qh_ref, ql_ref, arrived)
    steps = qh_ref.shape[0]
    for j in range(steps):
        started(block_copies(j, *halves))
    c = jnp.sum(parts_ref[...], axis=0, keepdims=True)
    c_ref[...] = c
    scale[...] = t_ref[...] / c
    total[...] = jnp.zeros_like(total)
    acc[...] = jnp.zeros_like(acc)
    inner = ((1,), (0,))
    wait(moves)
    depth = steps // 2 * BLOCK

    def scaled(j, carry):
        at = span(j, BLOCK)
        column = jnp.concatenate([as_column(scale[:, at])] * (w // 128), axis=1)
        yh, yl = split(y_ref[at, :] * column)
        half, k = j // (steps // 2), j % (steps // 2)
        yk[half, span(k, BLOCK), :] = yh
        yk[half, pl.ds(pl.multiple_of(depth + k * BLOCK, BLOCK), BLOCK), :] = yl
        yk[half, pl.ds(pl.multiple_of(2 * depth + k * BLOCK, BLOCK), BLOCK), :] = yh
        return carry

    lax.fori_loop(0, steps, scaled, 0)
    parts = acc.shape[0] // BLOCK

    def step(i, carry):
        half, rows = i // parts, span(i % parts, BLOCK)
        blocks = [half * (steps // 2) + k for k in range(steps // 2)]

        @pl.when(i % parts == 0)
        def _():
            for j in blocks:
                wait(block_copies(j, *halves))

        high = [qh_ref[j, rows, :] for j in blocks]
        low = [ql_ref[j, rows, :] for j in blocks]
        acc[rows, :] += dot(jnp.concatenate(high + high + low, axis=1), yk[half], inner)
        for j, a, b in zip(blocks, high, low):
            p = joint(a, b) * scale[:, span(j, BLOCK)]
            total[rows, :] += p[:, :128] + p[:, 128:]
        return carry

    lax.fori_loop(0, 2 * parts, step, 0)
    line[...] = lane_sums(total)
    for k in range(8):
        at = span(seats[k], 128)
        outs[k][:128, :] = acc[at, :]
        sums = jnp.concatenate([line[:, at]] * (w // 128), axis=1)
        outs[k][128:, :] = jnp.broadcast_to(sums, (8, w))


def noise_part_of(seats, qh, ql, parts, t, ys):
    n, m = qh.shape[1], qh.shape[0] * BLOCK
    w = ys[0].shape[1]
    out = call(
        noise_kernel,
        (parts, t),
        [f32(136, w)] * 8 + [f32(1, m)],
        (
            pltpu.VMEM((n, 128), jnp.float32),
            pltpu.VMEM((n, w), jnp.float32),
            pltpu.VMEM((2, 3 * m // 2, w), jnp.bfloat16),
            pltpu.VMEM((1, m), jnp.float32),
            pltpu.VMEM((1, n), jnp.float32),
            pltpu.VMEM((m, w), jnp.float32),
            pltpu.SemaphoreType.DMA((16,)),
            *matrix_scratch(n, m),
        ),
        flops=6 * n * m * w,
        far=(qh, ql, *ys),
        scalars=(seats,),
    )
    return out[:8], out[8]


def pairs(groups):
    return [p for a, b in groups for p in ((a, b), (b, a))]


def gathered(line, groups):
    n, size = line.shape[1], len(groups[0])
    mine = jnp.broadcast_to(line.reshape(1, n // 128, 128), (size, n // 128, 128))
    parts = lax.all_to_all(mine, ALL, 0, 0, axis_index_groups=groups, tiled=True)
    return parts.reshape(size, n)


def spread(own, ring, pair):
    across = pairs(pair)
    below = lax.ppermute(own, ring, UP)
    above = lax.ppermute(own, ring, DOWN)
    over = lax.ppermute(own, "y", across)
    far = lax.ppermute(below, ring, UP)
    over_below = lax.ppermute(over, ring, UP)
    over_above = lax.ppermute(over, ring, DOWN)
    over_far = lax.ppermute(far, "y", across)
    return [own, below, above, over, far, over_below, over_above, over_far]


def sum_to_owner(parts, ring, pair):
    own, up, far, down, over, over_up, over_far, over_down = parts
    across = pairs(pair)
    far = far + lax.ppermute(over_far, "y", across)
    over = over + lax.ppermute(over_up, ring, UP) + lax.ppermute(over_down, ring, DOWN)
    up = up + lax.ppermute(far, ring, UP)
    down = lax.ppermute(down, ring, DOWN)
    return own + down + lax.ppermute(over, "y", across) + lax.ppermute(up, ring, UP)


def shards(noise, data):
    iy, iz, ix, ic = (lax.axis_index(name) for name in ALL)
    row_y, col_y = iy % 2, iy // 2

    xs = spread(noise, "x", PAIRS_A)
    ys = spread(data, "z", PAIRS_B)
    ys = ys + [lax.ppermute(v, "c", CORES) for v in ys]

    hops = ((0, 0), (0, 3), (0, 1), (1, 0), (0, 2), (1, 3), (1, 1), (1, 2))
    row_slots = [(row_y ^ dy) * 4 + (ix + d) % 4 for dy, d in hops]
    col_slots = [(col_y ^ dy) * 4 + (iz + d) % 4 for dy, d in hops]
    slots = jnp.stack(
        row_slots + [ic * 8 + k for k in col_slots] + [(1 - ic) * 8 + k for k in col_slots]
    ).astype(jnp.int32)
    kk = jnp.arange(16, dtype=jnp.int32)
    row_order = ((kk[:8] // 4) ^ row_y) * 4 + (ix + kk[:8]) % 4
    col_seats = ((kk // 4 % 2) ^ col_y) * 4 + (kk - iz) % 4

    xt, s, row_lse, xn, yn = scores_of(slots, xs, ys)
    qh, ql, top, col_lse, a = columns_of(s, gathered(row_lse, SAME_ROWS))
    other = lax.ppermute(col_lse, "c", CORES)
    peak = jnp.maximum(col_lse, other)
    col_lse = peak + jnp.log2(1.0 + jnp.exp2(jnp.minimum(col_lse, other) - peak))
    row_part, t, b = row_sums(qh, ql, top, gathered(col_lse, SAME_COLUMNS))
    col_part, r = column_sums(qh, ql, gathered(row_part, SAME_ROWS), t)
    col_part = col_part + lax.ppermute(col_part, "c", CORES)
    to_other = data_part_of(1 - ic, col_seats, qh, ql, t, r, xt)
    to_own = data_part_of(ic, col_seats, qh, ql, t, r, xt)
    shares = [v + lax.ppermute(u, "c", CORES) for u, v in zip(to_other, to_own)]
    col_part, shares = lax.optimization_barrier((col_part, shares))
    col_parts = gathered(col_part, SAME_COLUMNS)
    data_sum = sum_to_owner(shares, "z", PAIRS_B)
    noise_part, c = noise_part_of(
        jnp.concatenate([row_order, slots[8:]]), qh, ql, col_parts, t, ys
    )
    noise_sum = sum_to_owner(noise_part, "x", PAIRS_A)
    noise_target = noise_sum[:128] / noise_sum[128, :128][:, None]
    mine = lax.dynamic_slice(c, (0, (ic * 8 + col_y * 4 + iz) * 128), (1, 128))
    data_target = data_sum / mine.reshape(128, 1)

    f = (xn + (LN2 * EPSILON) * (a - jnp.log2(r))).reshape(2, 4, 128)
    f_mine = lax.dynamic_index_in_dim(f, row_y, 0, keepdims=False)
    f_other = lax.ppermute(f_mine, "c", CORES)
    f_both = jnp.where(ic == 0, jnp.stack([f_mine, f_other], 1), jnp.stack([f_other, f_mine], 1))
    g = (yn + (LN2 * EPSILON) * (b - jnp.log2(c))).reshape(2, 2, 4, 128)
    g_mine = lax.dynamic_index_in_dim(g, ic, 0, keepdims=False)
    g_other = lax.ppermute(g_mine, "y", pairs(PAIRS_A))
    outer = (iy == 0) | (iy == 3)
    g_03, g_12 = jnp.where(outer, g_mine, g_other), jnp.where(outer, g_other, g_mine)
    g_all = jnp.stack([g_03[0], g_12[0], g_12[1], g_03[1]])
    return noise_target, data_target, f_both.reshape(-1), g_all.reshape(-1)


def solution(mesh):
    torus = Mesh(mesh.devices.reshape(4, 4, 4, 2), ALL)
    return jax.shard_map(
        shards,
        mesh=torus,
        in_specs=(P(("y", "z", "x", "c"), None), P(("x", "c", "y", "z"), None)),
        out_specs=(
            P(("y", "z", "x", "c"), None),
            P(("x", "c", "y", "z"), None),
            P(("y", "z")),
            P(("x", "c")),
        ),
        check_vma=False,
    )
```

```python
import functools

import jax
import jax.numpy as jnp
from jax import lax
from jax.experimental import pallas as pl
from jax.experimental.pallas import tpu as pltpu
from jax.sharding import Mesh
from jax.sharding import PartitionSpec as P

ALL = ("y", "z", "x", "c")
PAIRS_A = ((0, 1), (2, 3))
PAIRS_B = ((1, 2), (0, 3))
UP = [(i, (i + 1) % 4) for i in range(4)]
DOWN = [(i, (i - 1) % 4) for i in range(4)]
CORES = [(0, 1), (1, 0)]


def place(y, z, x, c):
    return ((y * 4 + z) * 4 + x) * 2 + c


SAME_ROWS = [
    [place(y, z, x, c) for y in pair for x in range(4)]
    for pair in PAIRS_A
    for z in range(4)
    for c in range(2)
]
SAME_COLUMNS = [
    [place(y, z, x, c) for y in pair for z in range(4)]
    for pair in PAIRS_B
    for x in range(4)
    for c in range(2)
]

EPSILON = 32.0
LOG2E = 1.4426950408889634
LN2 = 0.6931471805599453
SCALE = LOG2E / EPSILON
BLOCK = 256
WIDE = 512
TALL = 512
CHUNK = 64
VMEM_LIMIT = 32 * 1024 * 1024


SAME_COLUMNS_BOTH = [
    [place(y, z, x, c) for c in range(2) for y in pair for z in range(4)]
    for pair in PAIRS_B
    for x in range(4)
]


def split(v):
    high = v.astype(jnp.bfloat16)
    return high, (v - high.astype(jnp.float32)).astype(jnp.bfloat16)


def dot(a, b, dims):
    return lax.dot_general(a, b, (dims, ((), ())), preferred_element_type=jnp.float32)


def as_column(row):
    return jnp.broadcast_to(row, (128, row.shape[1])).T


def as_row(column):
    return column.T[0:1, :]


def call(
    kernel, arrays, out_shape, scratch=(), flops=0, transcendentals=0, scalars=(), far=(), far_out=0
):
    anywhere = pl.BlockSpec(memory_space=pltpu.HBM)
    vmem = pl.BlockSpec(memory_space=pltpu.VMEM)
    smem = pl.BlockSpec(memory_space=pltpu.SMEM)
    moved = sum(v.size * v.dtype.itemsize for v in (*far, *arrays, *out_shape))
    return pl.pallas_call(
        kernel,
        in_specs=[smem] * len(scalars) + [anywhere] * len(far) + [vmem] * len(arrays),
        out_specs=[anywhere] * far_out + [vmem] * (len(out_shape) - far_out),
        out_shape=[
            pltpu.HBM(v.shape, v.dtype) if k < far_out else v for k, v in enumerate(out_shape)
        ],
        scratch_shapes=scratch,
        cost_estimate=pl.CostEstimate(
            flops=flops, bytes_accessed=moved, transcendentals=transcendentals
        ),
        compiler_params=pltpu.CompilerParams(vmem_limit_bytes=VMEM_LIMIT),
    )(*scalars, *(pltpu.with_memory_space_constraint(v, pltpu.HBM) for v in far), *arrays)


def started(copies):
    for copy in copies:
        copy.start()
    return copies


def matrix_scratch(n, m):
    half = pltpu.VMEM((m // BLOCK, n, BLOCK), jnp.bfloat16)
    return half, half, pltpu.SemaphoreType.DMA((2, m // BLOCK))


def block_copies(j, high_from, low_from, high, low, arrived, first=0):
    return [
        pltpu.make_async_copy(a.at[first + j], b.at[j], arrived.at[side, j])
        for side, (a, b) in enumerate(((high_from, high), (low_from, low)))
    ]


def wait(copies):
    for copy in copies:
        copy.wait()


def store_for_all(ref, line):
    for k in range(ref.shape[1]):
        values = line[:, k * 128 : (k + 1) * 128]
        ref[:, k : k + 1, :] = jnp.broadcast_to(values.reshape(1, 1, 128), (ref.shape[0], 1, 128))


def span(k, size):
    return pl.ds(pl.multiple_of(k * size, size), size)


def f32(*shape):
    return jax.ShapeDtypeStruct(shape, jnp.float32)


def scores_kernel(*refs):
    slots, xs, ys = refs[0], refs[1:9], refs[9:25]
    xt_out, s_ref, lse_ref, xn_ref, yn_ref = refs[25:30]
    xk, yk, peak, total, x, y, xt, arrived, sent = refs[30:]
    n, m = s_ref.shape
    w = y.shape[1]
    steps = m // WIDE

    def norms(v):
        return as_row(jnp.broadcast_to(jnp.sum(v * v, axis=1, keepdims=True), (128, 128)))

    here = [(x if k < 8 else y).at[span(slots[k], 128)] for k in range(24)]
    copies = started(
        [
            pltpu.make_async_copy(a, b, arrived.at[k])
            for k, (a, b) in enumerate(zip((*xs, *ys), here))
        ]
    )
    wait(copies[:8])

    def place_row_block(k, carry):
        at = span(k, 128)
        v = x[at, :]
        xt[:, at] = v.T
        xn_ref[:, at] = norms(v)
        high, low = split(v * (2.0 * SCALE))
        xk[at, :w] = high
        xk[at, w : 2 * w] = high
        xk[at, 2 * w :] = low
        return carry

    lax.fori_loop(0, 8, place_row_block, 0)
    kept = pltpu.make_async_copy(xt, xt_out, sent)
    kept.start()
    wait(copies[8:])

    def prepare(j):
        for k in range(WIDE // 128):
            at = span(j * (WIDE // 128) + k, 128)
            v = y[at, :]
            yn_ref[:, at] = norms(v)
            high, low = split(v)
            yk[at, :w] = high
            yk[at, w : 2 * w] = low
            yk[at, 2 * w :] = high

    prepare(0)
    peak[...] = jnp.full_like(peak, -jnp.inf)
    total[...] = jnp.zeros_like(total)

    def multiply(j):
        at = span(j, WIDE)
        s_ref[:, at] = dot(xk[...], yk[at, :], ((1,), (1,)))

    def collect(j):
        at = span(j, WIDE)
        shift = SCALE * yn_ref[:, at]
        for i in range(0, n, CHUNK // 2):
            rows = slice(i, i + CHUNK // 2)
            t = s_ref[rows, at] - shift
            old = peak[rows, :]
            lanes = [t[:, k : k + 128] for k in range(0, WIDE, 128)]
            new = functools.reduce(jnp.maximum, lanes, old)
            part = sum(jnp.exp2(v - new) for v in lanes)
            total[rows, :] = total[rows, :] * jnp.exp2(old - new) + part
            peak[rows, :] = new

    multiply(0)
    prepare(1)

    def step(j, carry):
        multiply(j)
        collect(j - 1)
        prepare(jnp.minimum(j + 1, steps - 1))
        return carry

    lax.fori_loop(1, steps, step, 0)
    collect(steps - 1)
    top = jnp.max(peak[...], axis=1, keepdims=True)
    sums = jnp.sum(total[...] * jnp.exp2(peak[...] - top), axis=1, keepdims=True)
    store_for_all(lse_ref, as_row(jnp.broadcast_to(top + jnp.log2(sums), peak.shape)))
    kept.wait()


def scores_of(slots, xs, ys):
    n, m, w = 8 * 128, 16 * 128, xs[0].shape[1]
    return call(
        scores_kernel,
        (),
        (f32(w, n), f32(n, m), f32(8, n // 128, 128), f32(1, n), f32(1, m)),
        (
            pltpu.VMEM((n, 3 * w), jnp.bfloat16),
            pltpu.VMEM((m, 3 * w), jnp.bfloat16),
            pltpu.VMEM((n, 128), jnp.float32),
            pltpu.VMEM((n, 128), jnp.float32),
            pltpu.VMEM((n, w), jnp.float32),
            pltpu.VMEM((m, w), jnp.float32),
            pltpu.VMEM((w, n), jnp.float32),
            pltpu.SemaphoreType.DMA((24,)),
            pltpu.SemaphoreType.DMA,
        ),
        flops=6 * n * m * w,
        transcendentals=n * m,
        scalars=(slots,),
        far=(*xs, *ys),
        far_out=1,
    )


def negative_lse(parts):
    top = jnp.max(parts, axis=0, keepdims=True)
    return -(top + jnp.log2(jnp.sum(jnp.exp2(parts - top), axis=0, keepdims=True)))


def columns_kernel(
    s_ref, parts_ref, high_out, low_out, top_ref, lse_ref, a_ref, a_col, qh_ref, ql_ref, sent
):
    n, m = s_ref.shape
    a = negative_lse(parts_ref[...])
    a_ref[...] = a
    a_col[...] = as_column(a)

    def shifted(i, at):
        a = a_col[i : i + CHUNK, :]
        return s_ref[i : i + CHUNK, at] + jnp.concatenate([a] * (BLOCK // 128), axis=1)

    def folded(v, op):
        return op(v.reshape(CHUNK // 8, 8, BLOCK), axis=0)

    def step(j, carry):
        at = span(j, BLOCK)
        top = jnp.full((8, BLOCK), -jnp.inf, jnp.float32)
        for i in range(0, n, CHUNK):
            top = jnp.maximum(top, folded(shifted(i, at), jnp.max))
        top = jnp.max(top, axis=0, keepdims=True)
        total = jnp.zeros((8, BLOCK), jnp.float32)
        for i in range(0, n, CHUNK):
            q = jnp.exp2(shifted(i, at) - top)
            total = total + folded(q, jnp.sum)
            qh_ref[j, i : i + CHUNK, :], ql_ref[j, i : i + CHUNK, :] = split(q)
        top_ref[:, at] = top
        lse = top + jnp.log2(jnp.sum(total, axis=0, keepdims=True))
        for k in range(BLOCK // 128):
            values = lse[:, k * 128 : (k + 1) * 128].reshape(1, 1, 128)
            seat = pl.ds(j * (BLOCK // 128) + k, 1)
            lse_ref[:, seat, :] = jnp.broadcast_to(values, (lse_ref.shape[0], 1, 128))
        started(kept(j))
        return carry

    def kept(j):
        return [
            pltpu.make_async_copy(a.at[j], b.at[j], sent.at[side, j])
            for side, (a, b) in enumerate(((qh_ref, high_out), (ql_ref, low_out)))
        ]

    lax.fori_loop(0, m // BLOCK, step, 0)
    for j in range(m // BLOCK):
        wait(kept(j))


def columns_of(s, parts):
    n, m = s.shape
    half = jax.ShapeDtypeStruct((m // BLOCK, n, BLOCK), jnp.bfloat16)
    return call(
        columns_kernel,
        (s, parts),
        (half, half, f32(1, m), f32(16, m // 128, 128), f32(1, n)),
        (
            pltpu.VMEM((n, 128), jnp.float32),
            *matrix_scratch(n, m),
        ),
        flops=4 * n * m,
        transcendentals=n * m,
        far_out=2,
    )


def joint(high, low):
    return high.astype(jnp.float32) + low.astype(jnp.float32)


def add_weighted(total, high, low, weights):
    for i in range(0, total.shape[0], CHUNK):
        rows = slice(i, i + CHUNK)
        p = joint(high[rows, :], low[rows, :]) * weights
        total[rows, :] += p[:, :128] + p[:, 128:]


def lane_sums(total):
    return as_row(jnp.broadcast_to(jnp.sum(total[...], axis=1, keepdims=True), total.shape))


def rows_kernel(
    high, low, top_ref, parts_ref, sum_ref, t_ref, b_ref, total, qh_ref, ql_ref, arrived
):
    halves = (high, low, qh_ref, ql_ref, arrived)
    steps = qh_ref.shape[0]
    for j in range(steps):
        started(block_copies(j, *halves))
    b = negative_lse(parts_ref[...])
    b_ref[...] = b
    t_ref[...] = jnp.exp2(top_ref[...] + b)
    total[...] = jnp.zeros_like(total)

    def step(j, carry):
        wait(block_copies(j, *halves))
        add_weighted(total, qh_ref.at[j], ql_ref.at[j], t_ref[:, span(j, BLOCK)])
        return carry

    lax.fori_loop(0, steps, step, 0)
    store_for_all(sum_ref, lane_sums(total))


def row_sums(qh, ql, top, parts):
    n, m = qh.shape[1], qh.shape[0] * BLOCK
    return call(
        rows_kernel,
        (top, parts),
        (f32(8, n // 128, 128), f32(1, m), f32(1, m)),
        (pltpu.VMEM((n, 128), jnp.float32), *matrix_scratch(n, m)),
        flops=4 * n * m,
        far=(qh, ql),
    )


def column_sums_kernel(high, low, parts_ref, t_ref, sum_ref, r_ref, inv, qh_ref, ql_ref, arrived):
    halves = (high, low, qh_ref, ql_ref, arrived)
    steps = qh_ref.shape[0]
    for j in range(steps):
        started(block_copies(j, *halves))
    n = inv.shape[0]
    r = jnp.sum(parts_ref[...], axis=0, keepdims=True)
    r_ref[...] = r
    inv[...] = as_column(1.0 / r)

    def step(j, carry):
        wait(block_copies(j, *halves))
        total = jnp.zeros((8, BLOCK), jnp.float32)
        for i in range(0, n, CHUNK):
            rows = slice(i, i + CHUNK)
            scale = jnp.concatenate([inv[rows, :]] * (BLOCK // 128), axis=1)
            q = joint(qh_ref[j, rows, :], ql_ref[j, rows, :]) * scale
            total = total + jnp.sum(q.reshape(CHUNK // 8, 8, BLOCK), axis=0)
        at = span(j, BLOCK)
        sum_ref[:, at] = jnp.sum(total, axis=0, keepdims=True) * t_ref[:, at]
        return carry

    lax.fori_loop(0, steps, step, 0)


def column_sums(qh, ql, parts, t):
    n, m = qh.shape[1], qh.shape[0] * BLOCK
    return call(
        column_sums_kernel,
        (parts, t),
        (f32(1, m), f32(1, n)),
        (pltpu.VMEM((n, 128), jnp.float32), *matrix_scratch(n, m)),
        flops=4 * n * m,
        far=(qh, ql),
    )


def data_kernel(seats, high_from, low_from, xt_from, t_ref, r_ref, *refs):
    outs, (xt, xt_ref, come, qh_ref, ql_ref, arrived, done) = refs[:8], refs[8:]
    w = xt_ref.shape[0]
    steps = qh_ref.shape[0]
    first = pltpu.make_async_copy(xt_from, xt_ref, come)
    first.start()
    halves = (high_from, low_from, qh_ref, ql_ref, arrived, seats[0] * steps)
    for j in range(steps):
        started(block_copies(j, *halves))
    first.wait()
    high, low = split(xt_ref[...] * (1.0 / r_ref[...]))
    n = xt_ref.shape[1]
    xt[:, :n] = high
    xt[:, n : 2 * n] = low
    xt[:, 2 * n :] = high
    inner = ((1,), (0,))

    def step(j, carry):
        wait(block_copies(2 * j, *halves))
        wait(block_copies(2 * j + 1, *halves))
        scale = t_ref[:, span(seats[0] * (steps // 2) + j, 2 * BLOCK)]
        high = jnp.concatenate([qh_ref[2 * j], qh_ref[2 * j + 1]], axis=1)
        low = jnp.concatenate([ql_ref[2 * j], ql_ref[2 * j + 1]], axis=1)
        part = dot(xt[...], jnp.concatenate([high, high, low], axis=0), inner)
        part = (part * scale).T
        for k in range(2 * BLOCK // 128):
            done[seats[1 + j * (2 * BLOCK // 128) + k]] = part[k * 128 : (k + 1) * 128]
        return carry

    lax.fori_loop(0, steps // 2, step, 0)
    for k in range(8):
        outs[k][...] = done[k]


def data_part_of(core, seats, qh, ql, t, r, xt):
    n, m = qh.shape[1], qh.shape[0] * BLOCK
    w = xt.shape[0]
    return call(
        data_kernel,
        (t, r),
        [f32(128, w)] * 8,
        (
            pltpu.VMEM((w, 3 * n), jnp.bfloat16),
            pltpu.VMEM((w, n), jnp.float32),
            pltpu.SemaphoreType.DMA,
            *matrix_scratch(n, m // 2),
            pltpu.VMEM((8, 128, w), jnp.float32),
        ),
        flops=3 * n * m * w,
        far=(qh, ql, xt),
        scalars=(jnp.concatenate([core.reshape(1).astype(jnp.int32), seats]),),
    )


def noise_kernel(seats, high_from, low_from, *refs):
    ys, (parts_ref, t_ref), outs = refs[:16], refs[16:18], refs[18:26]
    c_ref, total, acc, yk, scale, line, y_ref, come, qh_ref, ql_ref, arrived = refs[26:]
    w = y_ref.shape[1]
    moves = started(
        [
            pltpu.make_async_copy(v, y_ref.at[span(seats[8 + k], 128)], come.at[k])
            for k, v in enumerate(ys)
        ]
    )
    halves = (high_from, low_from, qh_ref, ql_ref, arrived)
    steps = qh_ref.shape[0]
    for j in range(steps):
        started(block_copies(j, *halves))
    c = jnp.sum(parts_ref[...], axis=0, keepdims=True)
    c_ref[...] = c
    scale[...] = t_ref[...] / c
    total[...] = jnp.zeros_like(total)
    acc[...] = jnp.zeros_like(acc)
    inner = ((1,), (0,))
    wait(moves)
    depth = steps // 2 * BLOCK

    def scaled(j, carry):
        at = span(j, BLOCK)
        column = jnp.concatenate([as_column(scale[:, at])] * (w // 128), axis=1)
        yh, yl = split(y_ref[at, :] * column)
        half, k = j // (steps // 2), j % (steps // 2)
        yk[half, span(k, BLOCK), :] = yh
        yk[half, pl.ds(pl.multiple_of(depth + k * BLOCK, BLOCK), BLOCK), :] = yl
        yk[half, pl.ds(pl.multiple_of(2 * depth + k * BLOCK, BLOCK), BLOCK), :] = yh
        return carry

    lax.fori_loop(0, steps, scaled, 0)
    parts = acc.shape[0] // TALL

    def step(i, carry):
        half, rows = i // parts, span(i % parts, TALL)
        blocks = [half * (steps // 2) + k for k in range(steps // 2)]

        @pl.when(i % parts == 0)
        def _():
            for j in blocks:
                wait(block_copies(j, *halves))

        high = [qh_ref[j, rows, :] for j in blocks]
        low = [ql_ref[j, rows, :] for j in blocks]
        acc[rows, :] += dot(jnp.concatenate(high + high + low, axis=1), yk[half], inner)
        for j, a, b in zip(blocks, high, low):
            p = joint(a, b) * scale[:, span(j, BLOCK)]
            total[rows, :] += p[:, :128] + p[:, 128:]
        return carry

    lax.fori_loop(0, 2 * parts, step, 0)
    line[...] = lane_sums(total)
    for k in range(8):
        at = span(seats[k], 128)
        outs[k][:128, :] = acc[at, :]
        sums = jnp.concatenate([line[:, at]] * (w // 128), axis=1)
        outs[k][128:, :] = jnp.broadcast_to(sums, (8, w))


def noise_part_of(seats, qh, ql, parts, t, ys):
    n, m = qh.shape[1], qh.shape[0] * BLOCK
    w = ys[0].shape[1]
    out = call(
        noise_kernel,
        (parts, t),
        [f32(136, w)] * 8 + [f32(1, m)],
        (
            pltpu.VMEM((n, 128), jnp.float32),
            pltpu.VMEM((n, w), jnp.float32),
            pltpu.VMEM((2, 3 * m // 2, w), jnp.bfloat16),
            pltpu.VMEM((1, m), jnp.float32),
            pltpu.VMEM((1, n), jnp.float32),
            pltpu.VMEM((m, w), jnp.float32),
            pltpu.SemaphoreType.DMA((16,)),
            *matrix_scratch(n, m),
        ),
        flops=6 * n * m * w,
        far=(qh, ql, *ys),
        scalars=(seats,),
    )
    return out[:8], out[8]


def pairs(groups):
    return [p for a, b in groups for p in ((a, b), (b, a))]


def exchanged(mine, groups):
    parts = lax.all_to_all(mine, ALL, 0, 0, axis_index_groups=groups, tiled=True)
    return parts.reshape(parts.shape[0], -1)


def gathered(line, groups):
    n, size = line.shape[1], len(groups[0])
    return exchanged(jnp.broadcast_to(line.reshape(1, n // 128, 128), (size, n // 128, 128)), groups)


def spread(own, ring, pair):
    across = pairs(pair)
    below = lax.ppermute(own, ring, UP)
    above = lax.ppermute(own, ring, DOWN)
    over = lax.ppermute(own, "y", across)
    far = lax.ppermute(below, ring, UP)
    over_below = lax.ppermute(over, ring, UP)
    over_above = lax.ppermute(over, ring, DOWN)
    over_far = lax.ppermute(far, "y", across)
    return [own, below, above, over, far, over_below, over_above, over_far]


def sum_to_owner(parts, ring, pair):
    own, up, far, down, over, over_up, over_far, over_down = parts
    across = pairs(pair)
    far = far + lax.ppermute(over_far, "y", across)
    over = over + lax.ppermute(over_up, ring, UP) + lax.ppermute(over_down, ring, DOWN)
    up = up + lax.ppermute(far, ring, UP)
    down = lax.ppermute(down, ring, DOWN)
    return own + down + lax.ppermute(over, "y", across) + lax.ppermute(up, ring, UP)


def shards(noise, data):
    iy, iz, ix, ic = (lax.axis_index(name) for name in ALL)
    row_y, col_y = iy % 2, iy // 2

    xs = spread(noise, "x", PAIRS_A)
    ys = spread(data, "z", PAIRS_B)
    ys = ys + [lax.ppermute(v, "c", CORES) for v in ys]

    hops = ((0, 0), (0, 3), (0, 1), (1, 0), (0, 2), (1, 3), (1, 1), (1, 2))
    row_slots = [(row_y ^ dy) * 4 + (ix + d) % 4 for dy, d in hops]
    col_slots = [(col_y ^ dy) * 4 + (iz + d) % 4 for dy, d in hops]
    slots = jnp.stack(
        row_slots + [ic * 8 + k for k in col_slots] + [(1 - ic) * 8 + k for k in col_slots]
    ).astype(jnp.int32)
    kk = jnp.arange(16, dtype=jnp.int32)
    row_order = ((kk[:8] // 4) ^ row_y) * 4 + (ix + kk[:8]) % 4
    col_seats = ((kk // 4 % 2) ^ col_y) * 4 + (kk - iz) % 4

    xt, s, row_lse, xn, yn = scores_of(slots, xs, ys)
    qh, ql, top, col_lse, a = columns_of(s, exchanged(row_lse, SAME_ROWS))
    row_part, t, b = row_sums(qh, ql, top, exchanged(col_lse, SAME_COLUMNS_BOTH))
    col_part, r = column_sums(qh, ql, exchanged(row_part, SAME_ROWS), t)
    col_part = col_part + lax.ppermute(col_part, "c", CORES)
    to_other = data_part_of(1 - ic, col_seats, qh, ql, t, r, xt)
    to_own = data_part_of(ic, col_seats, qh, ql, t, r, xt)
    shares = [v + lax.ppermute(u, "c", CORES) for u, v in zip(to_other, to_own)]
    col_part, shares = lax.optimization_barrier((col_part, shares))
    col_parts = gathered(col_part, SAME_COLUMNS)
    data_sum = sum_to_owner(shares, "z", PAIRS_B)
    noise_part, c = noise_part_of(
        jnp.concatenate([row_order, slots[8:]]), qh, ql, col_parts, t, ys
    )
    noise_sum = sum_to_owner(noise_part, "x", PAIRS_A)
    noise_target = noise_sum[:128] / noise_sum[128, :128][:, None]
    mine = lax.dynamic_slice(c, (0, (ic * 8 + col_y * 4 + iz) * 128), (1, 128))
    data_target = data_sum / mine.reshape(128, 1)

    f = (xn + (LN2 * EPSILON) * (a - jnp.log2(r))).reshape(2, 4, 128)
    f_mine = lax.dynamic_index_in_dim(f, row_y, 0, keepdims=False)
    f_other = lax.ppermute(f_mine, "c", CORES)
    f_both = jnp.where(ic == 0, jnp.stack([f_mine, f_other], 1), jnp.stack([f_other, f_mine], 1))
    g = (yn + (LN2 * EPSILON) * (b - jnp.log2(c))).reshape(2, 2, 4, 128)
    g_mine = lax.dynamic_index_in_dim(g, ic, 0, keepdims=False)
    g_other = lax.ppermute(g_mine, "y", pairs(PAIRS_A))
    outer = (iy == 0) | (iy == 3)
    g_03, g_12 = jnp.where(outer, g_mine, g_other), jnp.where(outer, g_other, g_mine)
    g_all = jnp.stack([g_03[0], g_12[0], g_12[1], g_03[1]])
    return noise_target, data_target, f_both.reshape(-1), g_all.reshape(-1)


def solution(mesh):
    torus = Mesh(mesh.devices.reshape(4, 4, 4, 2), ALL)
    return jax.shard_map(
        shards,
        mesh=torus,
        in_specs=(P(("y", "z", "x", "c"), None), P(("x", "c", "y", "z"), None)),
        out_specs=(
            P(("y", "z", "x", "c"), None),
            P(("x", "c", "y", "z"), None),
            P(("y", "z")),
            P(("x", "c")),
        ),
        check_vma=False,
    )
```

```python
import functools

import jax
import jax.numpy as jnp
from jax import lax
from jax.experimental import pallas as pl
from jax.experimental.pallas import tpu as pltpu
from jax.sharding import Mesh
from jax.sharding import PartitionSpec as P

ALL = ("y", "z", "x", "c")
PAIRS_A = ((0, 1), (2, 3))
PAIRS_B = ((1, 2), (0, 3))
UP = [(i, (i + 1) % 4) for i in range(4)]
DOWN = [(i, (i - 1) % 4) for i in range(4)]
CORES = [(0, 1), (1, 0)]


def place(y, z, x, c):
    return ((y * 4 + z) * 4 + x) * 2 + c


SAME_ROWS = [
    [place(y, z, x, c) for y in pair for x in range(4)]
    for pair in PAIRS_A
    for z in range(4)
    for c in range(2)
]
SAME_COLUMNS = [
    [place(y, z, x, c) for y in pair for z in range(4)]
    for pair in PAIRS_B
    for x in range(4)
    for c in range(2)
]

EPSILON = 32.0
LOG2E = 1.4426950408889634
LN2 = 0.6931471805599453
SCALE = LOG2E / EPSILON
BLOCK = 256
WIDE = 512
TALL = 1024
CHUNK = 64
VMEM_LIMIT = 32 * 1024 * 1024


SAME_COLUMNS_BOTH = [
    [place(y, z, x, c) for c in range(2) for y in pair for z in range(4)]
    for pair in PAIRS_B
    for x in range(4)
]


def split(v):
    high = v.astype(jnp.bfloat16)
    return high, (v - high.astype(jnp.float32)).astype(jnp.bfloat16)


def dot(a, b, dims):
    return lax.dot_general(a, b, (dims, ((), ())), preferred_element_type=jnp.float32)


def as_column(row):
    return jnp.broadcast_to(row, (128, row.shape[1])).T


def as_row(column):
    return column.T[0:1, :]


def call(
    kernel, arrays, out_shape, scratch=(), flops=0, transcendentals=0, scalars=(), far=(), far_out=0
):
    anywhere = pl.BlockSpec(memory_space=pltpu.HBM)
    vmem = pl.BlockSpec(memory_space=pltpu.VMEM)
    smem = pl.BlockSpec(memory_space=pltpu.SMEM)
    moved = sum(v.size * v.dtype.itemsize for v in (*far, *arrays, *out_shape))
    return pl.pallas_call(
        kernel,
        in_specs=[smem] * len(scalars) + [anywhere] * len(far) + [vmem] * len(arrays),
        out_specs=[anywhere] * far_out + [vmem] * (len(out_shape) - far_out),
        out_shape=[
            pltpu.HBM(v.shape, v.dtype) if k < far_out else v for k, v in enumerate(out_shape)
        ],
        scratch_shapes=scratch,
        cost_estimate=pl.CostEstimate(
            flops=flops, bytes_accessed=moved, transcendentals=transcendentals
        ),
        compiler_params=pltpu.CompilerParams(vmem_limit_bytes=VMEM_LIMIT),
    )(*scalars, *(pltpu.with_memory_space_constraint(v, pltpu.HBM) for v in far), *arrays)


def started(copies):
    for copy in copies:
        copy.start()
    return copies


def matrix_scratch(n, m):
    half = pltpu.VMEM((m // BLOCK, n, BLOCK), jnp.bfloat16)
    return half, half, pltpu.SemaphoreType.DMA((2, m // BLOCK))


def block_copies(j, high_from, low_from, high, low, arrived, first=0):
    return [
        pltpu.make_async_copy(a.at[first + j], b.at[j], arrived.at[side, j])
        for side, (a, b) in enumerate(((high_from, high), (low_from, low)))
    ]


def wait(copies):
    for copy in copies:
        copy.wait()


def store_for_all(ref, line):
    for k in range(ref.shape[1]):
        values = line[:, k * 128 : (k + 1) * 128]
        ref[:, k : k + 1, :] = jnp.broadcast_to(values.reshape(1, 1, 128), (ref.shape[0], 1, 128))


def span(k, size):
    return pl.ds(pl.multiple_of(k * size, size), size)


def f32(*shape):
    return jax.ShapeDtypeStruct(shape, jnp.float32)


def scores_kernel(*refs):
    slots, xs, ys = refs[0], refs[1:9], refs[9:25]
    xt_out, s_ref, lse_ref, xn_ref, yn_ref = refs[25:30]
    xk, yk, peak, total, x, y, xt, arrived, sent = refs[30:]
    n, m = s_ref.shape
    w = y.shape[1]
    steps = m // WIDE

    def norms(v):
        return as_row(jnp.broadcast_to(jnp.sum(v * v, axis=1, keepdims=True), (128, 128)))

    here = [(x if k < 8 else y).at[span(slots[k], 128)] for k in range(24)]
    copies = started(
        [
            pltpu.make_async_copy(a, b, arrived.at[k])
            for k, (a, b) in enumerate(zip((*xs, *ys), here))
        ]
    )
    wait(copies[:8])

    def place_row_block(k, carry):
        at = span(k, 128)
        v = x[at, :]
        xt[:, at] = v.T
        xn_ref[:, at] = norms(v)
        high, low = split(v * (2.0 * SCALE))
        xk[at, :w] = high
        xk[at, w : 2 * w] = high
        xk[at, 2 * w :] = low
        return carry

    lax.fori_loop(0, 8, place_row_block, 0)
    kept = pltpu.make_async_copy(xt, xt_out, sent)
    kept.start()
    wait(copies[8:])

    def prepare(j):
        for k in range(WIDE // 128):
            at = span(j * (WIDE // 128) + k, 128)
            v = y[at, :]
            yn_ref[:, at] = norms(v)
            high, low = split(v)
            yk[at, :w] = high
            yk[at, w : 2 * w] = low
            yk[at, 2 * w :] = high

    prepare(0)
    peak[...] = jnp.full_like(peak, -jnp.inf)
    total[...] = jnp.zeros_like(total)

    def multiply(j):
        at = span(j, WIDE)
        s_ref[:, at] = dot(xk[...], yk[at, :], ((1,), (1,)))

    def collect(j):
        at = span(j, WIDE)
        shift = SCALE * yn_ref[:, at]
        for i in range(0, n, CHUNK // 2):
            rows = slice(i, i + CHUNK // 2)
            t = s_ref[rows, at] - shift
            old = peak[rows, :]
            lanes = [t[:, k : k + 128] for k in range(0, WIDE, 128)]
            new = functools.reduce(jnp.maximum, lanes, old)
            part = sum(jnp.exp2(v - new) for v in lanes)
            total[rows, :] = total[rows, :] * jnp.exp2(old - new) + part
            peak[rows, :] = new

    multiply(0)
    prepare(1)

    def step(j, carry):
        multiply(j)
        collect(j - 1)
        prepare(jnp.minimum(j + 1, steps - 1))
        return carry

    lax.fori_loop(1, steps, step, 0)
    collect(steps - 1)
    top = jnp.max(peak[...], axis=1, keepdims=True)
    sums = jnp.sum(total[...] * jnp.exp2(peak[...] - top), axis=1, keepdims=True)
    store_for_all(lse_ref, as_row(jnp.broadcast_to(top + jnp.log2(sums), peak.shape)))
    kept.wait()


def scores_of(slots, xs, ys):
    n, m, w = 8 * 128, 16 * 128, xs[0].shape[1]
    return call(
        scores_kernel,
        (),
        (f32(w, n), f32(n, m), f32(8, n // 128, 128), f32(1, n), f32(1, m)),
        (
            pltpu.VMEM((n, 3 * w), jnp.bfloat16),
            pltpu.VMEM((m, 3 * w), jnp.bfloat16),
            pltpu.VMEM((n, 128), jnp.float32),
            pltpu.VMEM((n, 128), jnp.float32),
            pltpu.VMEM((n, w), jnp.float32),
            pltpu.VMEM((m, w), jnp.float32),
            pltpu.VMEM((w, n), jnp.float32),
            pltpu.SemaphoreType.DMA((24,)),
            pltpu.SemaphoreType.DMA,
        ),
        flops=6 * n * m * w,
        transcendentals=n * m,
        scalars=(slots,),
        far=(*xs, *ys),
        far_out=1,
    )


def negative_lse(parts):
    top = jnp.max(parts, axis=0, keepdims=True)
    return -(top + jnp.log2(jnp.sum(jnp.exp2(parts - top), axis=0, keepdims=True)))


def columns_kernel(
    s_ref, parts_ref, high_out, low_out, top_ref, lse_ref, a_ref, a_col, qh_ref, ql_ref, sent
):
    n, m = s_ref.shape
    a = negative_lse(parts_ref[...])
    a_ref[...] = a
    a_col[...] = as_column(a)

    def shifted(i, at):
        a = a_col[i : i + CHUNK, :]
        return s_ref[i : i + CHUNK, at] + jnp.concatenate([a] * (BLOCK // 128), axis=1)

    def folded(v, op):
        return op(v.reshape(CHUNK // 8, 8, BLOCK), axis=0)

    def step(j, carry):
        at = span(j, BLOCK)
        top = jnp.full((8, BLOCK), -jnp.inf, jnp.float32)
        for i in range(0, n, CHUNK):
            top = jnp.maximum(top, folded(shifted(i, at), jnp.max))
        top = jnp.max(top, axis=0, keepdims=True)
        total = jnp.zeros((8, BLOCK), jnp.float32)
        for i in range(0, n, CHUNK):
            q = jnp.exp2(shifted(i, at) - top)
            total = total + folded(q, jnp.sum)
            qh_ref[j, i : i + CHUNK, :], ql_ref[j, i : i + CHUNK, :] = split(q)
        top_ref[:, at] = top
        lse = top + jnp.log2(jnp.sum(total, axis=0, keepdims=True))
        for k in range(BLOCK // 128):
            values = lse[:, k * 128 : (k + 1) * 128].reshape(1, 1, 128)
            seat = pl.ds(j * (BLOCK // 128) + k, 1)
            lse_ref[:, seat, :] = jnp.broadcast_to(values, (lse_ref.shape[0], 1, 128))
        started(kept(j))
        return carry

    def kept(j):
        return [
            pltpu.make_async_copy(a.at[j], b.at[j], sent.at[side, j])
            for side, (a, b) in enumerate(((qh_ref, high_out), (ql_ref, low_out)))
        ]

    lax.fori_loop(0, m // BLOCK, step, 0)
    for j in range(m // BLOCK):
        wait(kept(j))


def columns_of(s, parts):
    n, m = s.shape
    half = jax.ShapeDtypeStruct((m // BLOCK, n, BLOCK), jnp.bfloat16)
    return call(
        columns_kernel,
        (s, parts),
        (half, half, f32(1, m), f32(16, m // 128, 128), f32(1, n)),
        (
            pltpu.VMEM((n, 128), jnp.float32),
            *matrix_scratch(n, m),
        ),
        flops=4 * n * m,
        transcendentals=n * m,
        far_out=2,
    )


def joint(high, low):
    return high.astype(jnp.float32) + low.astype(jnp.float32)


def add_weighted(total, high, low, weights):
    for i in range(0, total.shape[0], CHUNK):
        rows = slice(i, i + CHUNK)
        p = joint(high[rows, :], low[rows, :]) * weights
        total[rows, :] += p[:, :128] + p[:, 128:]


def lane_sums(total):
    return as_row(jnp.broadcast_to(jnp.sum(total[...], axis=1, keepdims=True), total.shape))


def rows_kernel(
    high, low, top_ref, parts_ref, sum_ref, t_ref, b_ref, total, qh_ref, ql_ref, arrived
):
    halves = (high, low, qh_ref, ql_ref, arrived)
    steps = qh_ref.shape[0]
    for j in range(steps):
        started(block_copies(j, *halves))
    b = negative_lse(parts_ref[...])
    b_ref[...] = b
    t_ref[...] = jnp.exp2(top_ref[...] + b)
    total[...] = jnp.zeros_like(total)

    def step(j, carry):
        wait(block_copies(j, *halves))
        add_weighted(total, qh_ref.at[j], ql_ref.at[j], t_ref[:, span(j, BLOCK)])
        return carry

    lax.fori_loop(0, steps, step, 0)
    store_for_all(sum_ref, lane_sums(total))


def row_sums(qh, ql, top, parts):
    n, m = qh.shape[1], qh.shape[0] * BLOCK
    return call(
        rows_kernel,
        (top, parts),
        (f32(8, n // 128, 128), f32(1, m), f32(1, m)),
        (pltpu.VMEM((n, 128), jnp.float32), *matrix_scratch(n, m)),
        flops=4 * n * m,
        far=(qh, ql),
    )


def column_sums_kernel(high, low, parts_ref, t_ref, sum_ref, r_ref, inv, qh_ref, ql_ref, arrived):
    halves = (high, low, qh_ref, ql_ref, arrived)
    steps = qh_ref.shape[0]
    for j in range(steps):
        started(block_copies(j, *halves))
    n = inv.shape[0]
    r = jnp.sum(parts_ref[...], axis=0, keepdims=True)
    r_ref[...] = r
    inv[...] = as_column(1.0 / r)

    def step(j, carry):
        wait(block_copies(j, *halves))
        total = jnp.zeros((8, BLOCK), jnp.float32)
        for i in range(0, n, CHUNK):
            rows = slice(i, i + CHUNK)
            scale = jnp.concatenate([inv[rows, :]] * (BLOCK // 128), axis=1)
            q = joint(qh_ref[j, rows, :], ql_ref[j, rows, :]) * scale
            total = total + jnp.sum(q.reshape(CHUNK // 8, 8, BLOCK), axis=0)
        at = span(j, BLOCK)
        sum_ref[:, at] = jnp.sum(total, axis=0, keepdims=True) * t_ref[:, at]
        return carry

    lax.fori_loop(0, steps, step, 0)


def column_sums(qh, ql, parts, t):
    n, m = qh.shape[1], qh.shape[0] * BLOCK
    return call(
        column_sums_kernel,
        (parts, t),
        (f32(1, m), f32(1, n)),
        (pltpu.VMEM((n, 128), jnp.float32), *matrix_scratch(n, m)),
        flops=4 * n * m,
        far=(qh, ql),
    )


def data_kernel(seats, high_from, low_from, xt_from, t_ref, r_ref, *refs):
    outs, (xt, xt_ref, come, qh_ref, ql_ref, arrived, done) = refs[:8], refs[8:]
    w = xt_ref.shape[0]
    steps = qh_ref.shape[0]
    first = pltpu.make_async_copy(xt_from, xt_ref, come)
    first.start()
    halves = (high_from, low_from, qh_ref, ql_ref, arrived, seats[0] * steps)
    for j in range(steps):
        started(block_copies(j, *halves))
    first.wait()
    high, low = split(xt_ref[...] * (1.0 / r_ref[...]))
    n = xt_ref.shape[1]
    xt[:, :n] = high
    xt[:, n : 2 * n] = low
    xt[:, 2 * n :] = high
    inner = ((1,), (0,))

    def step(j, carry):
        wait(block_copies(2 * j, *halves))
        wait(block_copies(2 * j + 1, *halves))
        scale = t_ref[:, span(seats[0] * (steps // 2) + j, 2 * BLOCK)]
        high = jnp.concatenate([qh_ref[2 * j], qh_ref[2 * j + 1]], axis=1)
        low = jnp.concatenate([ql_ref[2 * j], ql_ref[2 * j + 1]], axis=1)
        part = dot(xt[...], jnp.concatenate([high, high, low], axis=0), inner)
        part = (part * scale).T
        for k in range(2 * BLOCK // 128):
            done[seats[1 + j * (2 * BLOCK // 128) + k]] = part[k * 128 : (k + 1) * 128]
        return carry

    lax.fori_loop(0, steps // 2, step, 0)
    for k in range(8):
        outs[k][...] = done[k]


def data_part_of(core, seats, qh, ql, t, r, xt):
    n, m = qh.shape[1], qh.shape[0] * BLOCK
    w = xt.shape[0]
    return call(
        data_kernel,
        (t, r),
        [f32(128, w)] * 8,
        (
            pltpu.VMEM((w, 3 * n), jnp.bfloat16),
            pltpu.VMEM((w, n), jnp.float32),
            pltpu.SemaphoreType.DMA,
            *matrix_scratch(n, m // 2),
            pltpu.VMEM((8, 128, w), jnp.float32),
        ),
        flops=3 * n * m * w,
        far=(qh, ql, xt),
        scalars=(jnp.concatenate([core.reshape(1).astype(jnp.int32), seats]),),
    )


def noise_kernel(seats, high_from, low_from, *refs):
    ys, (parts_ref, t_ref), outs = refs[:16], refs[16:18], refs[18:26]
    c_ref, total, acc, yk, scale, line, y_ref, come, qh_ref, ql_ref, arrived = refs[26:]
    w = y_ref.shape[1]
    moves = started(
        [
            pltpu.make_async_copy(v, y_ref.at[span(seats[8 + k], 128)], come.at[k])
            for k, v in enumerate(ys)
        ]
    )
    halves = (high_from, low_from, qh_ref, ql_ref, arrived)
    steps = qh_ref.shape[0]
    for j in range(steps):
        started(block_copies(j, *halves))
    c = jnp.sum(parts_ref[...], axis=0, keepdims=True)
    c_ref[...] = c
    scale[...] = t_ref[...] / c
    total[...] = jnp.zeros_like(total)
    acc[...] = jnp.zeros_like(acc)
    inner = ((1,), (0,))
    wait(moves)
    depth = steps // 2 * BLOCK

    def scaled(j, carry):
        at = span(j, BLOCK)
        column = jnp.concatenate([as_column(scale[:, at])] * (w // 128), axis=1)
        yh, yl = split(y_ref[at, :] * column)
        half, k = j // (steps // 2), j % (steps // 2)
        yk[half, span(k, BLOCK), :] = yh
        yk[half, pl.ds(pl.multiple_of(depth + k * BLOCK, BLOCK), BLOCK), :] = yl
        yk[half, pl.ds(pl.multiple_of(2 * depth + k * BLOCK, BLOCK), BLOCK), :] = yh
        return carry

    lax.fori_loop(0, steps, scaled, 0)
    parts = acc.shape[0] // TALL

    def step(i, carry):
        half, rows = i // parts, span(i % parts, TALL)
        blocks = [half * (steps // 2) + k for k in range(steps // 2)]

        @pl.when(i % parts == 0)
        def _():
            for j in blocks:
                wait(block_copies(j, *halves))

        high = [qh_ref[j, rows, :] for j in blocks]
        low = [ql_ref[j, rows, :] for j in blocks]
        acc[rows, :] += dot(jnp.concatenate(high + high + low, axis=1), yk[half], inner)
        for j, a, b in zip(blocks, high, low):
            p = joint(a, b) * scale[:, span(j, BLOCK)]
            total[rows, :] += p[:, :128] + p[:, 128:]
        return carry

    lax.fori_loop(0, 2 * parts, step, 0)
    line[...] = lane_sums(total)
    for k in range(8):
        at = span(seats[k], 128)
        outs[k][:128, :] = acc[at, :]
        sums = jnp.concatenate([line[:, at]] * (w // 128), axis=1)
        outs[k][128:, :] = jnp.broadcast_to(sums, (8, w))


def noise_part_of(seats, qh, ql, parts, t, ys):
    n, m = qh.shape[1], qh.shape[0] * BLOCK
    w = ys[0].shape[1]
    out = call(
        noise_kernel,
        (parts, t),
        [f32(136, w)] * 8 + [f32(1, m)],
        (
            pltpu.VMEM((n, 128), jnp.float32),
            pltpu.VMEM((n, w), jnp.float32),
            pltpu.VMEM((2, 3 * m // 2, w), jnp.bfloat16),
            pltpu.VMEM((1, m), jnp.float32),
            pltpu.VMEM((1, n), jnp.float32),
            pltpu.VMEM((m, w), jnp.float32),
            pltpu.SemaphoreType.DMA((16,)),
            *matrix_scratch(n, m),
        ),
        flops=6 * n * m * w,
        far=(qh, ql, *ys),
        scalars=(seats,),
    )
    return out[:8], out[8]


def pairs(groups):
    return [p for a, b in groups for p in ((a, b), (b, a))]


def exchanged(mine, groups):
    parts = lax.all_to_all(mine, ALL, 0, 0, axis_index_groups=groups, tiled=True)
    return parts.reshape(parts.shape[0], -1)


def gathered(line, groups):
    n, size = line.shape[1], len(groups[0])
    return exchanged(jnp.broadcast_to(line.reshape(1, n // 128, 128), (size, n // 128, 128)), groups)


def spread(own, ring, pair):
    across = pairs(pair)
    below = lax.ppermute(own, ring, UP)
    above = lax.ppermute(own, ring, DOWN)
    over = lax.ppermute(own, "y", across)
    far = lax.ppermute(below, ring, UP)
    over_below = lax.ppermute(over, ring, UP)
    over_above = lax.ppermute(over, ring, DOWN)
    over_far = lax.ppermute(far, "y", across)
    return [own, below, above, over, far, over_below, over_above, over_far]


def sum_to_owner(parts, ring, pair):
    own, up, far, down, over, over_up, over_far, over_down = parts
    across = pairs(pair)
    far = far + lax.ppermute(over_far, "y", across)
    over = over + lax.ppermute(over_up, ring, UP) + lax.ppermute(over_down, ring, DOWN)
    up = up + lax.ppermute(far, ring, UP)
    down = lax.ppermute(down, ring, DOWN)
    return own + down + lax.ppermute(over, "y", across) + lax.ppermute(up, ring, UP)


def shards(noise, data):
    iy, iz, ix, ic = (lax.axis_index(name) for name in ALL)
    row_y, col_y = iy % 2, iy // 2

    xs = spread(noise, "x", PAIRS_A)
    ys = spread(data, "z", PAIRS_B)
    ys = ys + [lax.ppermute(v, "c", CORES) for v in ys]

    hops = ((0, 0), (0, 3), (0, 1), (1, 0), (0, 2), (1, 3), (1, 1), (1, 2))
    row_slots = [(row_y ^ dy) * 4 + (ix + d) % 4 for dy, d in hops]
    col_slots = [(col_y ^ dy) * 4 + (iz + d) % 4 for dy, d in hops]
    slots = jnp.stack(
        row_slots + [ic * 8 + k for k in col_slots] + [(1 - ic) * 8 + k for k in col_slots]
    ).astype(jnp.int32)
    kk = jnp.arange(16, dtype=jnp.int32)
    row_order = ((kk[:8] // 4) ^ row_y) * 4 + (ix + kk[:8]) % 4
    col_seats = ((kk // 4 % 2) ^ col_y) * 4 + (kk - iz) % 4

    xt, s, row_lse, xn, yn = scores_of(slots, xs, ys)
    qh, ql, top, col_lse, a = columns_of(s, exchanged(row_lse, SAME_ROWS))
    row_part, t, b = row_sums(qh, ql, top, exchanged(col_lse, SAME_COLUMNS_BOTH))
    col_part, r = column_sums(qh, ql, exchanged(row_part, SAME_ROWS), t)
    col_part = col_part + lax.ppermute(col_part, "c", CORES)
    to_other = data_part_of(1 - ic, col_seats, qh, ql, t, r, xt)
    to_own = data_part_of(ic, col_seats, qh, ql, t, r, xt)
    shares = [v + lax.ppermute(u, "c", CORES) for u, v in zip(to_other, to_own)]
    col_part, shares = lax.optimization_barrier((col_part, shares))
    col_parts = gathered(col_part, SAME_COLUMNS)
    data_sum = sum_to_owner(shares, "z", PAIRS_B)
    noise_part, c = noise_part_of(
        jnp.concatenate([row_order, slots[8:]]), qh, ql, col_parts, t, ys
    )
    noise_sum = sum_to_owner(noise_part, "x", PAIRS_A)
    noise_target = noise_sum[:128] / noise_sum[128, :128][:, None]
    mine = lax.dynamic_slice(c, (0, (ic * 8 + col_y * 4 + iz) * 128), (1, 128))
    data_target = data_sum / mine.reshape(128, 1)

    f = (xn + (LN2 * EPSILON) * (a - jnp.log2(r))).reshape(2, 4, 128)
    f_mine = lax.dynamic_index_in_dim(f, row_y, 0, keepdims=False)
    f_other = lax.ppermute(f_mine, "c", CORES)
    f_both = jnp.where(ic == 0, jnp.stack([f_mine, f_other], 1), jnp.stack([f_other, f_mine], 1))
    g = (yn + (LN2 * EPSILON) * (b - jnp.log2(c))).reshape(2, 2, 4, 128)
    g_mine = lax.dynamic_index_in_dim(g, ic, 0, keepdims=False)
    g_other = lax.ppermute(g_mine, "y", pairs(PAIRS_A))
    outer = (iy == 0) | (iy == 3)
    g_03, g_12 = jnp.where(outer, g_mine, g_other), jnp.where(outer, g_other, g_mine)
    g_all = jnp.stack([g_03[0], g_12[0], g_12[1], g_03[1]])
    return noise_target, data_target, f_both.reshape(-1), g_all.reshape(-1)


def solution(mesh):
    torus = Mesh(mesh.devices.reshape(4, 4, 4, 2), ALL)
    return jax.shard_map(
        shards,
        mesh=torus,
        in_specs=(P(("y", "z", "x", "c"), None), P(("x", "c", "y", "z"), None)),
        out_specs=(
            P(("y", "z", "x", "c"), None),
            P(("x", "c", "y", "z"), None),
            P(("y", "z")),
            P(("x", "c")),
        ),
        check_vma=False,
    )
```
